128 devices in a mesh: dom: 128 (over z, y, x, core).
Axes of the slice: x: 4, y: 4, z: 4, core: 2. Of those that a mesh axis runs over, the one named last changes fastest.
Arguments:
- driving_force: float32 [10, 131072], P(None, 'dom'), may hold values from -8 to 8
- stiffness: float32 [131072], P('dom'), may hold values from 0.3 to 3
- coupling: float32 [131072], P('dom'), may hold values from 0.5 to 3
- friction: float32 [131072], P('dom'), may hold values from 0.2 to 5
- edge_coef: float32 [8, 131072], P(None, 'dom'), may hold values from 0.1 to 0.8
- neighbours: int32 [8, 131072], P(None, 'dom'), may hold values from 0 to 1535, as said below
- send_cells: int32 [512, 128], P('dom'), may hold values from 0 to 1023, as said below
- row_owner: int32 [16384, 1], P('dom'), may hold values from 0 to 127; in each aligned block of 128 rows (0 to 127, 128 to 255, ...) at most 2 rows name the same one
- pixel_cell: int32 [16384, 128], P('dom'), may hold values from 0 to 1023
- observed: float32 [16384, 128], P('dom'), may hold values from -6 to 6
- look_vector: float32 [2, 16384, 128], P(None, 'dom'), may hold values from -1 to 1
Outputs:
- velocity: float32 [10, 131072], P(None, 'dom')
- adjoint_state: float32 [10, 131072], P(None, 'dom')
- log_friction: float32 [131072], P('dom')
The draws below stay inside these ranges and needn't reach their ends.
Inputs may be any that keep to these rules, and one draw needn't show every extreme that they name: Column c of partition d's block lists cell c's neighbours: 5 to 8 live entries, each either another own cell (below 1024) or a received cell 1024 + j * 128 + h; the remaining entries equal c. Every received cell is named by some cell of the partition. `send_cells`: each list holds 128 distinct cells of its partition. `row_owner`: of the rows of one device, at most 2 name the same owner, and some device's block reaches this bound.
All inputs are finite; a program needn't handle non-finite values.
Results may differ from the reference program's by a relative error of at most 0.0001.
Values sent between devices are 32-bit elements; how exact they have to be, the bound alone decides.
A program may use at most 64 MiB of HBM per device.

```python
import math
import jax
import jax.numpy as jnp
import numpy as np

CELLS_DEV = 1024
HALO = 128
ROWS_DEV = 128
LAYERS = 5
SWEEPS = 4
STEPS = 2
NEIGHBOURS = 8
PARTNERS = 4
PIX = 128
DOMAINS = 128
CELLS = 131072
ROWS = 16384
CAP = 2


def draw_neighbours(key, part):
    device_count = CELLS // CELLS_DEV
    device_keys = jax.random.split(key, device_count)

    def one_device(device_key):
        key_degree, key_stride, key_order, key_extra, key_slot = jax.random.split(device_key, 5)
        column = jnp.arange(CELLS_DEV, dtype=jnp.int32)
        degree = jax.random.randint(key_degree, (CELLS_DEV,), 5, 9)
        stride = jax.random.randint(key_stride, (NEIGHBOURS, CELLS_DEV), 1, CELLS_DEV)
        local_entry = (column[None, :] + stride) % CELLS_DEV
        order_cells = jax.random.permutation(key_order, CELLS_DEV)
        slot_of_cell = jnp.zeros((CELLS_DEV,), jnp.int32).at[order_cells].set(column)
        entry_rank = jnp.arange(NEIGHBOURS, dtype=jnp.int32)[:, None]
        halo_slots = PARTNERS * HALO
        first_halo = (entry_rank == 0) & (slot_of_cell[None, :] < halo_slots)
        entry = jnp.where(first_halo, CELLS_DEV + slot_of_cell[None, :], local_entry)
        extra_pick = (entry_rank == 1) & (jax.random.randint(key_extra, (1, CELLS_DEV), 0, 4) == 0)
        extra_slot = CELLS_DEV + jax.random.randint(key_slot, (1, CELLS_DEV), 0, halo_slots)
        entry = jnp.where(extra_pick, extra_slot, entry)
        return jnp.where(entry_rank < degree[None, :], entry, column[None, :]).astype(jnp.int32)
    blocks = jax.vmap(one_device)(device_keys)
    return jnp.transpose(blocks, (1, 0, 2)).reshape(NEIGHBOURS, CELLS)


def draw_send_cells(key, part):
    list_keys = jax.random.split(key, PARTNERS * (CELLS // CELLS_DEV))

    def one_list(list_key):
        return jax.random.permutation(list_key, CELLS_DEV)[:HALO].astype(jnp.int32)
    return jax.vmap(one_list)(list_keys)


def place_ends(result, key, least, top_value):
    index_at = [jax.random.randint(jax.random.fold_in(key, axis), (), 0, length) for axis, length in enumerate(result.shape)]
    main_axis = result.shape.index(max(result.shape))
    neighbour = index_at[:main_axis] + [(index_at[main_axis] + 1) % result.shape[main_axis]] + index_at[main_axis + 1:]
    return result.at[tuple(index_at)].set(least).at[tuple(neighbour)].set(top_value)


def level_of(key, dims, cuts, least, top_value):
    def one(dim, parts):
        draws = jax.random.uniform(jax.random.fold_in(jax.random.fold_in(key, 6), dim), (parts,), jnp.float32, least / len(cuts), top_value / len(cuts))
        return jnp.repeat(jnp.exp(draws), dims[dim] // parts).reshape((-1,) + (1,) * (len(dims) - dim - 1))

    factor_of = one(*cuts[0])
    for cut in cuts[1:]:
        factor_of = factor_of * one(*cut)
    return factor_of


def deal_out(stream_key, own, number, rows, amount, top, most, skew):
    sequence = jax.random.permutation(stream_key, amount)
    crowded, ordinary = load_shares(amount, rows * top, most, skew, True), load_shares(amount, rows * top, most, skew, False)
    places = jnp.arange(amount)

    def named(sizes, rotation):
        used = int((sizes > 0).sum())
        fixed = max(1, used // 4)
        shifted = fixed + (places - fixed + rotation * (used - fixed)) % max(1, amount - fixed)
        return jnp.zeros((amount,), jnp.int32).at[sequence[jnp.where(places < fixed, places, shifted)]].set(jnp.asarray(sizes, jnp.int32))

    sizes = jnp.where(number % 4 == 0, named(crowded, number // 4), named(ordinary, number - number // 4 - 1))
    mixed = jax.random.permutation(jax.random.fold_in(own, 3), amount)
    source_of, sink = mixed[0:amount // 2 * 2:2], mixed[1:amount // 2 * 2:2]
    room = jnp.minimum(sizes[source_of] - 1, most - sizes[sink]) // 2
    room = jnp.where((source_of == sequence[0]) | (sink == sequence[0]) | (sizes[sink] == 0), 0, jnp.maximum(room, 0))
    shifted = jax.random.randint(jax.random.fold_in(own, 4), (amount // 2,), 0, 1 << 20) % (room + 1)
    sizes = sizes.at[source_of].add(-shifted).at[sink].add(shifted)
    items = jnp.searchsorted(jnp.cumsum(sizes), jnp.arange(rows * top), side="right").astype(jnp.int32)
    listing = items.reshape(top, rows).T
    listing = listing[jax.random.permutation(jax.random.fold_in(own, 1), rows)]
    rotation = jax.random.randint(jax.random.fold_in(own, 2), (rows, 1), 0, top)
    return jnp.take_along_axis(listing, (jnp.arange(top)[None, :] + rotation) % top, axis=1)


def load_shares(count, total, bound, lean, full):
    loads = [(1 << 20) // math.isqrt(grade ** lean) + 1 for grade in range(1, count + 1)]
    largest = bound if full else min(bound, max(-(-total // count), total * loads[0] // sum(loads)))
    least = 1 if total - largest >= count - 1 else 0
    counts, spare = [largest] + [least] * (count - 1), total - largest - least * (count - 1)
    while spare > 0:
        movable = [i for i in range(1, count) if counts[i] < largest] or [i for i in range(1, count) if counts[i] < bound]
        mass, remaining = sum([loads[i] for i in movable]), spare
        for i in movable:
            extra = min(bound - counts[i], max(1, remaining * loads[i] // mass), spare)
            counts[i] = counts[i] + extra
            spare = spare - extra
    return np.array(counts)


def bell_draw(own_key, dims, scale, most, pieces=(), kind=jnp.bfloat16):
    values = jax.random.normal(own_key, dims, jnp.float32) * scale
    if len(pieces) > 0:
        values = level_of(own_key, dims, pieces, -0.22, 0.18) * values
    return jnp.clip(values, min=-most, max=most).astype(kind)


def setup_inputs(seed: int = 0) -> dict:
    seeds = jax.random.split(jax.random.key(seed), 12)
    driving_force = bell_draw(seeds[0], (2 * LAYERS, CELLS), 3.0, 8.0, ((1, 128),), jnp.float32)
    stiffness = jnp.clip(jnp.exp(math.log(3.0) - 2.3025851 * jax.random.uniform(seeds[1], (CELLS,), jnp.float32) ** level_of(seeds[1], (CELLS,), ((0, 128),), -0.2, 0.2)), 0.3, 3.0)
    coupling = jnp.clip(jnp.exp(math.log(3.0) - 1.7917595 * jax.random.uniform(seeds[2], (CELLS,), jnp.float32) ** level_of(seeds[2], (CELLS,), ((0, 128),), -0.2, 0.2)), 0.5, 3.0)
    friction = jnp.clip(jnp.exp(math.log(5.0) - 3.218876 * jax.random.uniform(seeds[3], (CELLS,), jnp.float32) ** level_of(seeds[3], (CELLS,), ((0, 128),), -0.2, 0.2)), 0.2, 5.0)
    edge_coef = jnp.clip(jnp.exp(math.log(0.8) - 2.0794415 * jax.random.uniform(seeds[4], (NEIGHBOURS, CELLS), jnp.float32) ** level_of(seeds[4], (NEIGHBOURS, CELLS), ((1, 128),), -0.2, 0.2)), 0.1, 0.8)
    neighbours = draw_neighbours(jax.random.fold_in(seeds[11], 71), 0)
    send_cells = draw_send_cells(jax.random.fold_in(seeds[11], 71), 0)
    row_owner_keys = jax.random.split(jax.random.fold_in(seeds[7], 1), ROWS // ROWS_DEV)
    row_owner_turns = jax.random.permutation(jax.random.fold_in(seeds[7], 3), ROWS // ROWS_DEV)
    row_owner = jax.vmap(lambda own, number: deal_out(jax.random.fold_in(seeds[7], 2), own, number, ROWS_DEV, DOMAINS, 1, CAP, 2))(row_owner_keys, row_owner_turns).reshape((ROWS, 1))
    pixel_cell = place_ends(jax.random.randint(seeds[8], (ROWS, PIX), 0, CELLS_DEV), jax.random.fold_in(seeds[8], 1), 0, CELLS_DEV - 1).astype(jnp.int32)
    observed = bell_draw(seeds[9], (ROWS, PIX), 1.0, 6.0, ((0, 128),), jnp.float32)
    look_vector = jnp.clip(jax.random.uniform(seeds[10], (2, ROWS, PIX), jnp.float32, -1.0, 1.0) * level_of(seeds[10], (2, ROWS, PIX), ((1, 128),), -0.4, 0.0), -1.0, 1.0)
    return dict(driving_force=driving_force, stiffness=stiffness, coupling=coupling, friction=friction, edge_coef=edge_coef, neighbours=neighbours, send_cells=send_cells, row_owner=row_owner, pixel_cell=pixel_cell, observed=observed, look_vector=look_vector)


partner_offsets = (1, -1, 2, -2)
step_rate = 0.5


def global_lists(neighbours, send_cells):
    column = jnp.arange(CELLS, dtype=jnp.int32)
    device = column // CELLS_DEV
    local_own = column % CELLS_DEV
    beyond = neighbours - CELLS_DEV
    slot_number = jnp.clip(beyond // HALO, 0, PARTNERS - 1).astype(jnp.int32)
    position = jnp.clip(beyond % HALO, 0, HALO - 1).astype(jnp.int32)
    offset_table = jnp.array(partner_offsets, dtype=jnp.int32)
    source = (device[None, :] - offset_table[slot_number]) % DOMAINS
    remote = send_cells[source * PARTNERS + slot_number, position] + source * CELLS_DEV
    inside = neighbours < CELLS_DEV
    global_index = jnp.where(inside, device[None, :] * CELLS_DEV + neighbours, remote).astype(jnp.int32)
    live_entry = neighbours != local_own[None, :]
    return global_index, live_entry


def vertical_sum(current, coupling):
    shaped = current.reshape(2, LAYERS, -1)
    zero_layer = jnp.zeros_like(shaped[:, :1])
    from_above = jnp.concatenate([zero_layer, shaped[:, :-1]], axis=1)
    from_below = jnp.concatenate([shaped[:, 1:], zero_layer], axis=1)
    return (coupling[None, None, :] * (from_above + from_below)).reshape(2 * LAYERS, -1)


def diagonal_of(stiffness, coupling, rowsum, friction_now):
    layer_index = jnp.arange(LAYERS)
    top_flag = (layer_index == 0).astype(jnp.float32)
    base_flag = (layer_index == LAYERS - 1).astype(jnp.float32)
    link_count = 2.0 - top_flag - base_flag
    base_diag = stiffness[None, :] + rowsum[None, :] + coupling[None, :] * link_count[:, None] + friction_now[None, :] * base_flag[:, None]
    return jnp.concatenate([base_diag, base_diag], axis=0)


def reference(driving_force, stiffness, coupling, friction, edge_coef, neighbours, send_cells, row_owner, pixel_cell, observed, look_vector):
    global_index, live_entry = global_lists(neighbours, send_cells)
    weights = jnp.where(live_entry, edge_coef, 0.0)
    rowsum = jnp.sum(weights, axis=0)
    pixel_global = (row_owner[:, :1] * CELLS_DEV + pixel_cell).reshape(-1).astype(jnp.int32)
    obs_flat = observed.reshape(-1)
    look_x = look_vector[0].reshape(-1)
    look_y = look_vector[1].reshape(-1)
    log_friction = jnp.log(friction)
    velocity = jnp.zeros_like(driving_force)
    adjoint_state = jnp.zeros_like(driving_force)
    for outer_step in range(STEPS):
        diagonal = diagonal_of(stiffness, coupling, rowsum, jnp.exp(log_friction))
        for sweep_number in range(SWEEPS):
            across = jnp.zeros_like(driving_force)
            for entry_number in range(NEIGHBOURS):
                across = across + weights[entry_number][None, :] * velocity[:, global_index[entry_number]]
            velocity = (driving_force + across + vertical_sum(velocity, coupling)) / diagonal
        mean_speed = velocity.reshape(2, LAYERS, -1).mean(axis=1)
        misfit = look_x * mean_speed[0][pixel_global] + look_y * mean_speed[1][pixel_global] - obs_flat
        pull_x = jax.ops.segment_sum(look_x * misfit, pixel_global, num_segments=CELLS)
        pull_y = jax.ops.segment_sum(look_y * misfit, pixel_global, num_segments=CELLS)
        source_term = jnp.repeat(jnp.stack([pull_x, pull_y]) / LAYERS, LAYERS, axis=0)
        adjoint_state = jnp.zeros_like(driving_force)
        for sweep_number in range(SWEEPS):
            gathered = jnp.zeros_like(driving_force)
            for entry_number in range(NEIGHBOURS):
                gathered = gathered.at[:, global_index[entry_number]].add(weights[entry_number][None, :] * adjoint_state)
            adjoint_state = (source_term + gathered + vertical_sum(adjoint_state, coupling)) / diagonal
        gradient = -(adjoint_state[LAYERS - 1] * velocity[LAYERS - 1] + adjoint_state[2 * LAYERS - 1] * velocity[2 * LAYERS - 1])
        log_friction = log_friction - step_rate * jnp.tanh(jnp.exp(log_friction) * gradient)
    return velocity, adjoint_state, log_friction
```

```python
import jax
import jax.numpy as jnp
from jax import lax
from jax.experimental import pallas as pl
from jax.experimental.pallas import tpu as pltpu
from jax.sharding import PartitionSpec as P

SWEEPS = 4
STEPS = 2
OFFSETS = (1, -1, 2, -2)
RATE = 0.5
LAYERS = 5
ROUNDS = 13
MESH = pl.DeviceIdType.MESH
NT = (((1,), (1,)), ((), ()))
NN = (((1,), (0,)), ((), ()))
f32 = jnp.float32
bf16 = jnp.bfloat16


def split(x):
    hi = x.astype(bf16).astype(f32)
    return hi, x - hi


def stacked(x):
    hi, lo = split(x)
    return jnp.concatenate([hi, lo], axis=0).astype(bf16)


def mm(a, b, dims):
    return lax.dot_general(a, b, dims, preferred_element_type=f32)


def body(
    drv, stiff, coup, fric, edge, nbr, send, got,
    vel_out, adj_out, lf_out,
    mhi, mlo, sel, frc, wts, sums, snd, rcv, ssem, rsem,
):
    n = lax.axis_size("dom")
    me = lax.axis_index("dom")
    cells = drv.shape[1]
    halo = send.shape[1]
    ext = cells + 4 * halo

    barrier = pltpu.get_barrier_semaphore()
    for o in OFFSETS:
        pl.semaphore_signal(
            barrier, inc=1, device_id=(lax.rem(me + o + n, n),), device_id_type=MESH
        )

    col = lax.broadcasted_iota(jnp.int32, (8, cells), 1)
    weights = jnp.where(nbr[...] != col, edge[...], 0.0)
    wts[...] = weights
    rowsum = jnp.sum(weights, axis=0, keepdims=True)
    layer = lax.broadcasted_iota(jnp.int32, (8, cells), 0)
    links = jnp.where((layer == 0) | (layer == LAYERS - 1), 1.0, 2.0)
    coupling = coup[...]
    static_diag = stiff[...] + rowsum + coupling * links

    frc[...] = jnp.zeros_like(frc)
    frc[0:LAYERS, :] = drv[0:LAYERS, :]
    frc[8 : 8 + LAYERS, :] = drv[LAYERS : 2 * LAYERS, :]

    def inverse(lf):
        diag = static_diag + jnp.where(layer == LAYERS - 1, jnp.exp(lf), 0.0)
        return jnp.where(layer < LAYERS, 1.0 / diag, 0.0)

    def scaled(x, inv):
        return jnp.concatenate([x[0:8] * inv, x[8:16] * inv], axis=0)

    def vertical(x):
        return coupling * (pltpu.roll(x, 1, 0) + pltpu.roll(x, 15, 0))

    for j in range(4):
        rows = lax.broadcasted_iota(jnp.int32, (cells, halo), 0)
        hit = rows == send[j : j + 1, :]
        sel[:, j * halo : (j + 1) * halo] = jnp.where(hit, 1.0, 0.0).astype(bf16)

    def build(b, carry):
        base = pl.multiple_of(b * 128, 128)
        rows = lax.broadcasted_iota(jnp.int32, (128, cells), 0) + base
        acc = jnp.zeros((128, cells), f32)
        for e in range(8):
            acc = acc + jnp.where(rows == nbr[e : e + 1, :], wts[e : e + 1, :], 0.0)
        hi, lo = split(acc)
        mhi[pl.ds(base, 128), :] = hi.astype(bf16)
        mlo[pl.ds(base, 128), :] = lo.astype(bf16)
        return carry

    lax.fori_loop(0, ext // 128, build, 0)

    def pixels(g, acc):
        lhs = []
        rhs = []
        for s in range(4):
            blk = got[g * 4 + s]
            for slot in range(2):
                idx = blk[slot : slot + 1].astype(jnp.int32)
                ob = blk[2 + slot : 3 + slot]
                lx = blk[4 + slot : 5 + slot]
                ly = blk[6 + slot : 7 + slot]
                low = lax.broadcasted_iota(jnp.int32, (128, 128), 0) == (idx & 127)
                rhs.append(jnp.where(low, 1.0, 0.0).astype(bf16))
                high = lax.broadcasted_iota(jnp.int32, (8, 128), 0) == (idx >> 7)
                vals = [
                    jnp.where(high, q, 0.0)
                    for q in (lx * lx, lx * ly, ly * ly, lx * ob, ly * ob)
                ]
                lhs.append(stacked(jnp.concatenate(vals, axis=0)))
        return acc + mm(jnp.concatenate(lhs, axis=1), jnp.concatenate(rhs, axis=1), NT)

    acc = lax.fori_loop(0, got.shape[0] // 4, pixels, jnp.zeros((80, 128), f32))
    tot = acc[0:40] + acc[40:80]
    for q in range(5):
        for h in range(8):
            sums[q : q + 1, h * 128 : (h + 1) * 128] = tot[q * 8 + h : q * 8 + h + 1]

    pl.semaphore_wait(barrier, 4)

    def copies(i, sign):
        return [
            pltpu.make_async_remote_copy(
                snd.at[i, j],
                rcv.at[i, j],
                ssem.at[i, j],
                rsem.at[i, j],
                device_id=(lax.rem(me + sign * o + n, n),),
                device_id_type=MESH,
            )
            for j, o in enumerate(OFFSETS)
        ]

    def fetched(i):
        return jnp.concatenate([rcv[i, j] for j in range(4)], axis=1)

    def fwd(i, x, inv):
        xs = stacked(x)
        piece = mm(xs, sel[...], NN)
        piece = piece[0:16] + piece[16:32]
        cps = copies(i, 1)
        for j in range(4):
            snd[i, j] = piece[:, j * halo : (j + 1) * halo]
            cps[j].start()
        a = mm(xs, mhi[0:cells, :], NN)
        own = a[0:16] + a[16:32] + mm(xs[0:16], mlo[0:cells, :], NN)
        own = own + frc[...] + vertical(x)
        for c in cps:
            c.wait_recv()
        ys = stacked(fetched(i))
        a = mm(ys, mhi[cells:ext, :], NN)
        own = own + a[0:16] + a[16:32] + mm(ys[0:16], mlo[cells:ext, :], NN)
        return scaled(own, inv)

    def adj(i, x, source, inv):
        xs = stacked(x)
        a = mm(xs, mhi[cells:ext, :], NT)
        piece = a[0:16] + a[16:32] + mm(xs[0:16], mlo[cells:ext, :], NT)
        cps = copies(i, -1)
        for j in range(4):
            snd[i, j] = piece[:, j * halo : (j + 1) * halo]
            cps[j].start()
        a = mm(xs, mhi[0:cells, :], NT)
        own = a[0:16] + a[16:32] + mm(xs[0:16], mlo[0:cells, :], NT)
        own = own + source + vertical(x)
        for c in cps:
            c.wait_recv()
        ys = stacked(fetched(i))
        a = mm(ys, sel[...], NT)
        own = own + a[0:16] + a[16:32]
        return scaled(own, inv)

    lf = jnp.log(fric[...])
    first = 0
    x = None
    for step in range(STEPS):
        inv = inverse(lf)
        if step == 0:
            x = scaled(frc[...], inv)
            count = SWEEPS - 1
        else:
            count = SWEEPS
        x = lax.fori_loop(first, first + count, lambda i, v: fwd(i, v, inv), x)
        first += count
        mx = jnp.sum(x[0:8], axis=0, keepdims=True) / LAYERS
        my = jnp.sum(x[8:16], axis=0, keepdims=True) / LAYERS
        px = (sums[0:1, :] * mx + sums[1:2, :] * my - sums[3:4, :]) / LAYERS
        py = (sums[1:2, :] * mx + sums[2:3, :] * my - sums[4:5, :]) / LAYERS
        source = jnp.concatenate(
            [jnp.broadcast_to(px, (8, cells)), jnp.broadcast_to(py, (8, cells))], axis=0
        )
        lam = scaled(source, inv)
        lam = lax.fori_loop(
            first, first + SWEEPS - 1, lambda i, v: adj(i, v, source, inv), lam
        )
        first += SWEEPS - 1
        grad = -(lam[4:5] * x[4:5] + lam[12:13] * x[12:13])
        lf = lf - RATE * jnp.tanh(jnp.exp(lf) * grad)

    vel_out[0:LAYERS, :] = x[0:LAYERS]
    vel_out[LAYERS : 2 * LAYERS, :] = x[8 : 8 + LAYERS]
    adj_out[0:LAYERS, :] = lam[0:LAYERS]
    adj_out[LAYERS : 2 * LAYERS, :] = lam[8 : 8 + LAYERS]
    lf_out[...] = lf

    def drain(i, carry):
        for c in copies(i, 1):
            c.wait_send()
        return carry

    lax.fori_loop(0, ROUNDS, drain, 0)


def local(
    driving_force, stiffness, coupling, friction, edge_coef, neighbours,
    send_cells, row_owner, pixel_cell, observed, look_vector,
):
    n = lax.axis_size("dom")
    cells = driving_force.shape[1]
    halo = send_cells.shape[1]
    ext = cells + 4 * halo
    owners = row_owner[:, 0]
    rows = owners.shape[0]
    order = jnp.arange(rows, dtype=jnp.int32)
    earlier = (owners[:, None] == owners[None, :]) & (order[None, :] < order[:, None])
    slot = owners * 2 + jnp.sum(earlier, axis=1).astype(jnp.int32)
    place = (jnp.arange(2 * n, dtype=jnp.int32)[:, None] == slot[None, :]).astype(f32)
    payload = jnp.stack(
        [pixel_cell.astype(f32), observed, look_vector[0], look_vector[1]], axis=1
    )
    out = jnp.dot(place, payload.reshape(rows, -1), precision=lax.Precision.HIGHEST)
    out = out.reshape(n, 2, 4, -1).transpose(0, 2, 1, 3).reshape(n, 8, -1)
    got = lax.all_to_all(out, "dom", split_axis=0, concat_axis=0, tiled=True)

    vmem = pl.BlockSpec(memory_space=pltpu.VMEM)
    vel, adj, lf = pl.pallas_call(
        body,
        out_shape=(
            jax.ShapeDtypeStruct(driving_force.shape, f32),
            jax.ShapeDtypeStruct(driving_force.shape, f32),
            jax.ShapeDtypeStruct((1, cells), f32),
        ),
        in_specs=[vmem] * 8,
        out_specs=(vmem, vmem, vmem),
        scratch_shapes=[
            pltpu.VMEM((ext, cells), bf16),
            pltpu.VMEM((ext, cells), bf16),
            pltpu.VMEM((cells, 4 * halo), bf16),
            pltpu.VMEM((16, cells), f32),
            pltpu.VMEM((8, cells), f32),
            pltpu.VMEM((8, cells), f32),
            pltpu.VMEM((ROUNDS, 4, 16, halo), f32),
            pltpu.VMEM((ROUNDS, 4, 16, halo), f32),
            pltpu.SemaphoreType.DMA((ROUNDS, 4)),
            pltpu.SemaphoreType.DMA((ROUNDS, 4)),
        ],
        compiler_params=pltpu.CompilerParams(
            collective_id=0, has_side_effects=True, vmem_limit_bytes=48 * 1024 * 1024
        ),
    )(
        driving_force, stiffness[None, :], coupling[None, :], friction[None, :],
        edge_coef, neighbours, send_cells, got,
    )
    return vel, adj, lf[0]


def solution(mesh):
    in_specs = (
        P(None, "dom"), P("dom"), P("dom"), P("dom"), P(None, "dom"), P(None, "dom"),
        P("dom", None), P("dom", None), P("dom", None), P("dom", None), P(None, "dom", None),
    )
    out_specs = (P(None, "dom"), P(None, "dom"), P("dom"))
    return jax.shard_map(local, mesh=mesh, in_specs=in_specs, out_specs=out_specs, check_vma=False)
```

```python
import jax
import jax.numpy as jnp
from jax import lax
from jax.experimental import pallas as pl
from jax.experimental.pallas import tpu as pltpu
from jax.sharding import PartitionSpec as P

SWEEPS = 4
STEPS = 2
OFFSETS = (1, -1, 2, -2)
ORDER = (2, 3, 0, 1)
RATE = 0.5
LAYERS = 5
ROUNDS = 13
MESH = pl.DeviceIdType.MESH
NT = (((1,), (1,)), ((), ()))
NN = (((1,), (0,)), ((), ()))
f32 = jnp.float32
bf16 = jnp.bfloat16


def split(x):
    hi = x.astype(bf16).astype(f32)
    return hi, x - hi


def stacked(x):
    hi, lo = split(x)
    return jnp.concatenate([hi, lo], axis=0).astype(bf16)


def mm(a, b, dims=NN):
    return lax.dot_general(a, b, dims, preferred_element_type=f32)


def iota(shape, dim):
    return lax.broadcasted_iota(jnp.int32, shape, dim)


def body(
    drv, stiff, coup, fric, edge, nbr, send, owner, pcell, obs, look,
    vel_out, adj_out, lf_out,
    mhi, mlo, thi, tlo, sel, selt, frc, wts, sums, out, got, snd, rcv,
    ssem, rsem, asem, gsem,
):
    n = lax.axis_size("dom")
    me = lax.axis_index("dom")
    cells = drv.shape[1]
    halo = send.shape[1]
    ext = cells + 4 * halo

    barrier = pltpu.get_barrier_semaphore()

    def greet(r, carry):
        pl.semaphore_signal(
            barrier, inc=1, device_id=(lax.rem(me + r, n),), device_id_type=MESH
        )
        return carry

    lax.fori_loop(1, n, greet, 0)

    weights = jnp.where(nbr[...] != iota((8, cells), 1), edge[...], 0.0)
    wts[...] = weights
    rowsum = jnp.sum(weights, axis=0, keepdims=True)
    layer = iota((8, cells), 0)
    links = jnp.where((layer == 0) | (layer == LAYERS - 1), 1.0, 2.0)
    coupling = coup[...]
    static_diag = stiff[...] + rowsum + coupling * links

    frc[...] = jnp.zeros_like(frc)
    frc[0:LAYERS, :] = drv[0:LAYERS, :]
    frc[8 : 8 + LAYERS, :] = drv[LAYERS : 2 * LAYERS, :]

    def inverse(lf):
        diag = static_diag + jnp.where(layer == LAYERS - 1, jnp.exp(lf), 0.0)
        return jnp.where(layer < LAYERS, 1.0 / diag, 0.0)

    def scaled(x, inv):
        return jnp.concatenate([x[0:8] * inv, x[8:16] * inv], axis=0)

    def vertical(x):
        return coupling * (pltpu.roll(x, 1, 0) + pltpu.roll(x, 15, 0))

    for j in range(4):
        hit = iota((cells, halo), 0) == send[j : j + 1, :]
        sel[:, j * halo : (j + 1) * halo] = jnp.where(hit, 1.0, 0.0).astype(bf16)

    own_col = owner[...].astype(f32)
    eye = iota((128, 128), 0) == iota((128, 128), 1)
    own_row = jnp.sum(jnp.where(eye, own_col, 0.0), axis=0, keepdims=True)
    before = (own_col == own_row) & (iota((128, 128), 0) < iota((128, 128), 1))
    rank = jnp.sum(jnp.where(before, 1.0, 0.0), axis=0, keepdims=True)
    first_line = (own_row * 8.0 + rank).astype(jnp.int32)
    lines = jnp.concatenate([first_line + 2 * q for q in range(4)], axis=1)
    data = jnp.concatenate(
        [pcell[...].astype(f32), obs[...], look[0], look[1]], axis=0
    )
    hi, lo = split(data)
    data = jnp.concatenate([hi, lo], axis=1).astype(bf16)
    for b in range(8):
        hit = iota((128, 512), 0) + 128 * b == lines
        placed = mm(jnp.where(hit, 1.0, 0.0).astype(bf16), data)
        placed = placed[:, 0:128] + placed[:, 128:256]
        out[b * 16 : (b + 1) * 16] = placed.reshape(16, 8, 128)

    def build(b, carry):
        base = pl.multiple_of(b * 128, 128)
        rows = iota((128, cells), 0) + base
        acc = jnp.zeros((128, cells), f32)
        for e in range(8):
            acc = acc + jnp.where(rows == nbr[e : e + 1, :], wts[e : e + 1, :], 0.0)
        hi, lo = split(acc)
        mhi[pl.ds(base, 128), :] = hi.astype(bf16)
        mlo[pl.ds(base, 128), :] = lo.astype(bf16)
        return carry

    def row_copy(r):
        peer = lax.rem(me + r, n)
        return pltpu.make_async_remote_copy(
            out.at[peer], got.at[me], asem.at[0], gsem.at[0],
            device_id=(peer,), device_id_type=MESH,
        )

    def row_start(r, carry):
        row_copy(r).start()
        return carry

    def rows_done(sem, ref):
        all_but_one = ref.at[pl.ds(0, n - 1)]
        pltpu.make_async_copy(all_but_one, all_but_one, sem.at[0]).wait()

    def pixels(g, acc):
        lhs = []
        rhs = []
        for s in range(4):
            blk = got[g * 4 + s]
            for slot in range(2):
                idx = blk[slot : slot + 1].astype(jnp.int32)
                ob = blk[2 + slot : 3 + slot]
                lx = blk[4 + slot : 5 + slot]
                ly = blk[6 + slot : 7 + slot]
                low = iota((128, 128), 0) == (idx & 127)
                rhs.append(jnp.where(low, 1.0, 0.0).astype(bf16))
                high = iota((8, 128), 0) == (idx >> 7)
                vals = [
                    jnp.where(high, q, 0.0)
                    for q in (lx * lx, lx * ly, ly * ly, lx * ob, ly * ob)
                ]
                lhs.append(stacked(jnp.concatenate(vals, axis=0)))
        return acc + mm(jnp.concatenate(lhs, axis=1), jnp.concatenate(rhs, axis=1), NT)

    def copies(i, sign):
        return [
            pltpu.make_async_remote_copy(
                snd.at[i, j],
                rcv.at[i, j],
                ssem.at[i, j],
                rsem.at[i, j],
                device_id=(lax.rem(me + sign * o + n, n),),
                device_id_type=MESH,
            )
            for j, o in enumerate(OFFSETS)
        ]

    def push(i, piece, sign):
        cps = copies(i, sign)
        for j in ORDER:
            snd[i, j] = piece[:, j * halo : (j + 1) * halo]
            cps[j].start()

    def fetched(i, sign):
        for c in copies(i, sign):
            c.wait_recv()
        return stacked(jnp.concatenate([rcv[i, j] for j in range(4)], axis=1))

    def two(xs, hi, lo, dims=NN):
        a = mm(xs, hi, dims)
        return a[0:16] + a[16:32] + mm(xs[0:16], lo, dims)

    def fwd_send(i, xs):
        piece = mm(xs, sel[...])
        push(i, piece[0:16] + piece[16:32], 1)

    def fwd_own(xs):
        return two(xs, mhi[0:cells, :], mlo[0:cells, :])

    def fwd_halo(i):
        return two(fetched(i, 1), mhi[cells:ext, :], mlo[cells:ext, :])

    def fwd(i, x, inv, extra=None):
        xs = stacked(x)
        fwd_send(i, xs)
        if extra is not None:
            extra()
        own = fwd_own(xs) + frc[...] + vertical(x)
        return scaled(own + fwd_halo(i), inv)

    def adj(i, x, source, inv, extra=None):
        xs = stacked(x)
        push(i, two(xs, thi[...], tlo[...]), -1)
        if extra is not None:
            extra()
        own = two(xs, mhi[0:cells, :], mlo[0:cells, :], NT) + source + vertical(x)
        a = mm(fetched(i, -1), selt[...])
        return scaled(own + a[0:16] + a[16:32], inv)

    pl.semaphore_wait(barrier, n - 1)

    lf = jnp.log(fric[...])
    inv = inverse(lf)
    x = scaled(frc[...], inv)

    def during_first():
        lax.fori_loop(1, n, row_start, 0)
        got[me] = out[me]
        lax.fori_loop(0, ext // 128, build, 0)

    def during_second():
        thi[...] = mhi[cells:ext, :].astype(f32).T.astype(bf16)
        tlo[...] = mlo[cells:ext, :].astype(f32).T.astype(bf16)
        selt[...] = sel[...].astype(f32).T.astype(bf16)

    def during_third():
        rows_done(gsem, got)
        acc = lax.fori_loop(0, n // 4, pixels, jnp.zeros((80, 128), f32))
        tot = acc[0:40] + acc[40:80]
        for q in range(5):
            for h in range(8):
                line = q * 8 + h
                sums[q : q + 1, h * 128 : (h + 1) * 128] = tot[line : line + 1]

    x = fwd(0, x, inv, during_first)
    x = fwd(1, x, inv, during_second)
    x = fwd(2, x, inv, during_third)

    def source_of(x):
        mx = jnp.sum(x[0:8], axis=0, keepdims=True) / LAYERS
        my = jnp.sum(x[8:16], axis=0, keepdims=True) / LAYERS
        px = (sums[0:1, :] * mx + sums[1:2, :] * my - sums[3:4, :]) / LAYERS
        py = (sums[1:2, :] * mx + sums[2:3, :] * my - sums[4:5, :]) / LAYERS
        return jnp.concatenate(
            [jnp.broadcast_to(px, (8, cells)), jnp.broadcast_to(py, (8, cells))], axis=0
        )

    def stepped(lf, lam, x):
        grad = -(lam[4:5] * x[4:5] + lam[12:13] * x[12:13])
        return lf - RATE * jnp.tanh(jnp.exp(lf) * grad)

    source = source_of(x)
    lam = scaled(source, inv)
    held = []

    def early_send():
        fwd_send(6, stacked(x))

    def early_across():
        held.append(fwd_own(stacked(x)) + fwd_halo(6) + frc[...] + vertical(x))

    lam = adj(3, lam, source, inv, early_send)
    lam = adj(4, lam, source, inv, early_across)
    lam = adj(5, lam, source, inv)
    lf = stepped(lf, lam, x)

    inv = inverse(lf)
    x = scaled(held[0], inv)
    x = lax.fori_loop(7, 10, lambda i, v: fwd(i, v, inv), x)
    source = source_of(x)
    lam = scaled(source, inv)
    vel_out[0:LAYERS, :] = x[0:LAYERS]
    vel_out[LAYERS : 2 * LAYERS, :] = x[8 : 8 + LAYERS]
    lam = lax.fori_loop(10, 13, lambda i, v: adj(i, v, source, inv), lam)
    lf = stepped(lf, lam, x)

    adj_out[0:LAYERS, :] = lam[0:LAYERS]
    adj_out[LAYERS : 2 * LAYERS, :] = lam[8 : 8 + LAYERS]
    lf_out[...] = lf

    def drain(i, carry):
        for c in copies(i, 1):
            c.wait_send()
        return carry

    lax.fori_loop(0, ROUNDS, drain, 0)
    rows_done(asem, out)


def local(
    driving_force, stiffness, coupling, friction, edge_coef, neighbours,
    send_cells, row_owner, pixel_cell, observed, look_vector,
):
    n = lax.axis_size("dom")
    cells = driving_force.shape[1]
    halo = send_cells.shape[1]
    ext = cells + 4 * halo
    vmem = pl.BlockSpec(memory_space=pltpu.VMEM)
    vel, adj, lf = pl.pallas_call(
        body,
        out_shape=(
            jax.ShapeDtypeStruct(driving_force.shape, f32),
            jax.ShapeDtypeStruct(driving_force.shape, f32),
            jax.ShapeDtypeStruct((1, cells), f32),
        ),
        in_specs=[vmem] * 11,
        out_specs=(vmem, vmem, vmem),
        scratch_shapes=[
            pltpu.VMEM((ext, cells), bf16),
            pltpu.VMEM((ext, cells), bf16),
            pltpu.VMEM((cells, 4 * halo), bf16),
            pltpu.VMEM((cells, 4 * halo), bf16),
            pltpu.VMEM((cells, 4 * halo), bf16),
            pltpu.VMEM((4 * halo, cells), bf16),
            pltpu.VMEM((16, cells), f32),
            pltpu.VMEM((8, cells), f32),
            pltpu.VMEM((8, cells), f32),
            pltpu.VMEM((n, 8, 128), f32),
            pltpu.VMEM((n, 8, 128), f32),
            pltpu.VMEM((ROUNDS, 4, 16, halo), f32),
            pltpu.VMEM((ROUNDS, 4, 16, halo), f32),
            pltpu.SemaphoreType.DMA((ROUNDS, 4)),
            pltpu.SemaphoreType.DMA((ROUNDS, 4)),
            pltpu.SemaphoreType.DMA((1,)),
            pltpu.SemaphoreType.DMA((1,)),
        ],
        compiler_params=pltpu.CompilerParams(
            collective_id=0, has_side_effects=True, vmem_limit_bytes=48 * 1024 * 1024
        ),
    )(
        driving_force, stiffness[None, :], coupling[None, :], friction[None, :],
        edge_coef, neighbours, send_cells, row_owner, pixel_cell, observed, look_vector,
    )
    return vel, adj, lf[0]


def solution(mesh):
    in_specs = (
        P(None, "dom"), P("dom"), P("dom"), P("dom"), P(None, "dom"), P(None, "dom"),
        P("dom", None), P("dom", None), P("dom", None), P("dom", None), P(None, "dom", None),
    )
    out_specs = (P(None, "dom"), P(None, "dom"), P("dom"))
    return jax.shard_map(local, mesh=mesh, in_specs=in_specs, out_specs=out_specs, check_vma=False)
```

```python
import jax
import jax.numpy as jnp
from jax import lax
from jax.experimental import pallas as pl
from jax.experimental.pallas import tpu as pltpu
from jax.sharding import PartitionSpec as P

SWEEPS = 4
STEPS = 2
OFFSETS = (1, -1, 2, -2)
ORDER = (2, 3, 0, 1)
RATE = 0.5
LAYERS = 5
ROUNDS = 13
MESH = pl.DeviceIdType.MESH
NT = (((1,), (1,)), ((), ()))
NN = (((1,), (0,)), ((), ()))
f32 = jnp.float32
bf16 = jnp.bfloat16


def split(x):
    hi = x.astype(bf16).astype(f32)
    return hi, x - hi


def stacked(x):
    hi, lo = split(x)
    return jnp.concatenate([hi, lo], axis=0).astype(bf16)


def mm(a, b, dims=NN):
    return lax.dot_general(a, b, dims, preferred_element_type=f32)


def iota(shape, dim):
    return lax.broadcasted_iota(jnp.int32, shape, dim)


def place_of(part):
    core = lax.rem(part, 2)
    chip = lax.div(part, 2)
    x = lax.rem(chip, 4)
    y = lax.rem(lax.div(chip, 4), 4)
    z = lax.div(chip, 16)
    x = x + lax.rem(y, 2) * (3 - 2 * x)
    y = y + lax.rem(z, 2) * (3 - 2 * y)
    return ((z * 4 + y) * 4 + x) * 2 + 1 - core


def part_at(device):
    core = lax.rem(device, 2)
    chip = lax.div(device, 2)
    x = lax.rem(chip, 4)
    y = lax.rem(lax.div(chip, 4), 4)
    z = lax.div(chip, 16)
    y = y + lax.rem(z, 2) * (3 - 2 * y)
    x = x + lax.rem(y, 2) * (3 - 2 * x)
    return ((z * 4 + y) * 4 + x) * 2 + 1 - core


def body(
    drv_in, stiff_in, coup_in, fric_in, edge_in, nbr_in, send_in,
    owner_in, pcell_in, obs_in, look_in,
    vel_out, adj_out, lf_out,
    drv, stiff, coup, fric, edge, nbr, send, owner, pcell, obs, look,
    vel, adjoint, logf,
    mhi, mlo, thi, tlo, sel, selt, frc, wts, sums, out, got, snd, rcv,
    ssem, rsem, asem, gsem, lsem, msem, isem, osem, hsem,
):
    n = lax.axis_size("dom")
    me = lax.axis_index("dom")
    mine = part_at(me)
    away = place_of(me)
    cells = drv.shape[1]
    halo = send.shape[1]
    ext = cells + 4 * halo

    loads = [
        pltpu.make_async_copy(src, dst, lsem.at[k])
        for k, (src, dst) in enumerate(
            [(owner_in, owner), (pcell_in, pcell), (obs_in, obs), (look_in, look)]
        )
    ]
    for c in loads:
        c.start()
    moves = [
        pltpu.make_async_remote_copy(
            src, dst, msem.at[k], isem.at[k], device_id=(away,), device_id_type=MESH
        )
        for k, (src, dst) in enumerate(
            [
                (send_in, send), (nbr_in, nbr), (edge_in, edge), (stiff_in, stiff),
                (coup_in, coup), (fric_in, fric), (drv_in, drv),
            ]
        )
    ]
    partners = [
        [place_of(lax.rem(mine + sign * o + n, n)) for o in OFFSETS] for sign in (1, -1)
    ]

    barrier = pltpu.get_barrier_semaphore()

    def greet(r, carry):
        pl.semaphore_signal(
            barrier, inc=1, device_id=(lax.rem(me + r, n),), device_id_type=MESH
        )
        return carry

    lax.fori_loop(1, n, greet, 0)

    for c in loads:
        c.wait()
    own_row = owner[...].astype(f32)
    eye = iota((128, 128), 0) == iota((128, 128), 1)
    own_col = jnp.sum(jnp.where(eye, own_row, 0.0), axis=1, keepdims=True)
    before = (own_col == own_row) & (iota((128, 128), 0) < iota((128, 128), 1))
    rank = jnp.sum(jnp.where(before, 1.0, 0.0), axis=0, keepdims=True)
    first_line = (own_row * 8.0 + rank).astype(jnp.int32)
    lines = jnp.concatenate([first_line + 2 * q for q in range(4)], axis=1)
    data = jnp.concatenate(
        [pcell[...].astype(f32), obs[...], look[0], look[1]], axis=0
    )
    hi, lo = split(data)
    data = jnp.concatenate([hi, lo], axis=1).astype(bf16)
    for b in range(8):
        hit = iota((128, 512), 0) + 128 * b == lines
        placed = mm(jnp.where(hit, 1.0, 0.0).astype(bf16), data)
        placed = placed[:, 0:128] + placed[:, 128:256]
        out[b * 16 : (b + 1) * 16] = placed.reshape(16, 8, 128)

    pl.semaphore_wait(barrier, n - 1)
    for c in moves:
        c.start()

    def row_copy(r):
        peer = lax.rem(me + r, n)
        return pltpu.make_async_remote_copy(
            out.at[part_at(peer)], got.at[me], asem.at[0], gsem.at[0],
            device_id=(peer,), device_id_type=MESH,
        )

    def row_start(r, carry):
        row_copy(r).start()
        return carry

    lax.fori_loop(1, n, row_start, 0)
    got[me] = out[mine]
    for c in moves:
        c.wait_recv()

    weights = jnp.where(nbr[...] != iota((8, cells), 1), edge[...], 0.0)
    wts[...] = weights
    rowsum = jnp.sum(weights, axis=0, keepdims=True)
    layer = iota((8, cells), 0)
    links = jnp.where((layer == 0) | (layer == LAYERS - 1), 1.0, 2.0)
    coupling = coup[...]
    static_diag = stiff[...] + rowsum + coupling * links

    frc[...] = jnp.zeros_like(frc)
    frc[0:LAYERS, :] = drv[0:LAYERS, :]
    frc[8 : 8 + LAYERS, :] = drv[LAYERS : 2 * LAYERS, :]

    def inverse(lf):
        diag = static_diag + jnp.where(layer == LAYERS - 1, jnp.exp(lf), 0.0)
        return jnp.where(layer < LAYERS, 1.0 / diag, 0.0)

    def scaled(x, inv):
        return jnp.concatenate([x[0:8] * inv, x[8:16] * inv], axis=0)

    def vertical(x):
        return coupling * (pltpu.roll(x, 1, 0) + pltpu.roll(x, 15, 0))

    for j in range(4):
        hit = iota((cells, halo), 0) == send[j : j + 1, :]
        sel[:, j * halo : (j + 1) * halo] = jnp.where(hit, 1.0, 0.0).astype(bf16)

    def build(b, carry):
        base = pl.multiple_of(b * 128, 128)
        rows = iota((128, cells), 0) + base
        acc = jnp.zeros((128, cells), f32)
        for e in range(8):
            acc = acc + jnp.where(rows == nbr[e : e + 1, :], wts[e : e + 1, :], 0.0)
        hi, lo = split(acc)
        mhi[pl.ds(base, 128), :] = hi.astype(bf16)
        mlo[pl.ds(base, 128), :] = lo.astype(bf16)
        return carry

    def rows_done(sem, ref):
        all_but_one = ref.at[pl.ds(0, n - 1)]
        pltpu.make_async_copy(all_but_one, all_but_one, sem.at[0]).wait()

    def pixels(g, acc):
        lhs = []
        rhs = []
        for s in range(4):
            blk = got[g * 4 + s]
            for slot in range(2):
                idx = blk[slot : slot + 1].astype(jnp.int32)
                ob = blk[2 + slot : 3 + slot]
                lx = blk[4 + slot : 5 + slot]
                ly = blk[6 + slot : 7 + slot]
                low = iota((128, 128), 0) == (idx & 127)
                rhs.append(jnp.where(low, 1.0, 0.0).astype(bf16))
                high = iota((8, 128), 0) == (idx >> 7)
                vals = [
                    jnp.where(high, q, 0.0)
                    for q in (lx * lx, lx * ly, ly * ly, lx * ob, ly * ob)
                ]
                lhs.append(stacked(jnp.concatenate(vals, axis=0)))
        return acc + mm(jnp.concatenate(lhs, axis=1), jnp.concatenate(rhs, axis=1), NT)

    def copies(i, sign):
        return [
            pltpu.make_async_remote_copy(
                snd.at[i, j],
                rcv.at[i, j],
                ssem.at[i, j],
                rsem.at[i, j],
                device_id=(partners[0 if sign == 1 else 1][j],),
                device_id_type=MESH,
            )
            for j in range(4)
        ]

    def push(i, piece, sign):
        cps = copies(i, sign)
        for j in ORDER:
            snd[i, j] = piece[:, j * halo : (j + 1) * halo]
            cps[j].start()

    def fetched(i, sign):
        for c in copies(i, sign):
            c.wait_recv()
        return stacked(jnp.concatenate([rcv[i, j] for j in range(4)], axis=1))

    def two(xs, hi, lo, dims=NN):
        a = mm(xs, hi, dims)
        return a[0:16] + a[16:32] + mm(xs[0:16], lo, dims)

    def fwd_send(i, xs):
        piece = mm(xs, sel[...])
        push(i, piece[0:16] + piece[16:32], 1)

    def fwd_own(xs):
        return two(xs, mhi[0:cells, :], mlo[0:cells, :])

    def fwd_halo(i):
        return two(fetched(i, 1), mhi[cells:ext, :], mlo[cells:ext, :])

    def fwd(i, x, inv, extra=None):
        xs = stacked(x)
        fwd_send(i, xs)
        if extra is not None:
            extra()
        own = fwd_own(xs) + frc[...] + vertical(x)
        return scaled(own + fwd_halo(i), inv)

    def adj(i, x, source, inv, extra=None):
        xs = stacked(x)
        push(i, two(xs, thi[...], tlo[...]), -1)
        if extra is not None:
            extra()
        own = two(xs, mhi[0:cells, :], mlo[0:cells, :], NT) + source + vertical(x)
        a = mm(fetched(i, -1), selt[...])
        return scaled(own + a[0:16] + a[16:32], inv)

    lf = jnp.log(fric[...])
    inv = inverse(lf)
    x = scaled(frc[...], inv)

    def during_first():
        lax.fori_loop(0, ext // 128, build, 0)

    def during_second():
        thi[...] = mhi[cells:ext, :].astype(f32).T.astype(bf16)
        tlo[...] = mlo[cells:ext, :].astype(f32).T.astype(bf16)
        selt[...] = sel[...].astype(f32).T.astype(bf16)

    def during_third():
        rows_done(gsem, got)
        acc = lax.fori_loop(0, n // 4, pixels, jnp.zeros((80, 128), f32))
        tot = acc[0:40] + acc[40:80]
        for q in range(5):
            for h in range(8):
                line = q * 8 + h
                sums[q : q + 1, h * 128 : (h + 1) * 128] = tot[line : line + 1]

    x = fwd(0, x, inv, during_first)
    x = fwd(1, x, inv, during_second)
    x = fwd(2, x, inv, during_third)

    def source_of(x):
        mx = jnp.sum(x[0:8], axis=0, keepdims=True) / LAYERS
        my = jnp.sum(x[8:16], axis=0, keepdims=True) / LAYERS
        px = (sums[0:1, :] * mx + sums[1:2, :] * my - sums[3:4, :]) / LAYERS
        py = (sums[1:2, :] * mx + sums[2:3, :] * my - sums[4:5, :]) / LAYERS
        return jnp.concatenate(
            [jnp.broadcast_to(px, (8, cells)), jnp.broadcast_to(py, (8, cells))], axis=0
        )

    def stepped(lf, lam, x):
        grad = -(lam[4:5] * x[4:5] + lam[12:13] * x[12:13])
        return lf - RATE * jnp.tanh(jnp.exp(lf) * grad)

    homeward = [
        pltpu.make_async_remote_copy(
            src, dst, osem.at[k], hsem.at[k], device_id=(mine,), device_id_type=MESH
        )
        for k, (src, dst) in enumerate([(vel, vel_out), (adjoint, adj_out), (logf, lf_out)])
    ]

    source = source_of(x)
    lam = scaled(source, inv)
    held = []

    def early_send():
        fwd_send(6, stacked(x))

    def early_across():
        held.append(fwd_own(stacked(x)) + fwd_halo(6) + frc[...] + vertical(x))

    lam = adj(3, lam, source, inv, early_send)
    lam = adj(4, lam, source, inv, early_across)
    lam = adj(5, lam, source, inv)
    lf = stepped(lf, lam, x)

    inv = inverse(lf)
    x = scaled(held[0], inv)
    x = lax.fori_loop(7, 10, lambda i, v: fwd(i, v, inv), x)
    source = source_of(x)
    lam = scaled(source, inv)
    vel[0:LAYERS, :] = x[0:LAYERS]
    vel[LAYERS : 2 * LAYERS, :] = x[8 : 8 + LAYERS]
    homeward[0].start()
    lam = lax.fori_loop(10, 13, lambda i, v: adj(i, v, source, inv), lam)
    lf = stepped(lf, lam, x)

    adjoint[0:LAYERS, :] = lam[0:LAYERS]
    adjoint[LAYERS : 2 * LAYERS, :] = lam[8 : 8 + LAYERS]
    homeward[1].start()
    logf[...] = lf
    homeward[2].start()

    def drain(i, carry):
        for c in copies(i, 1):
            c.wait_send()
        return carry

    lax.fori_loop(0, ROUNDS, drain, 0)
    rows_done(asem, out)
    for c in moves:
        c.wait_send()
    for c in homeward:
        c.wait()


def local(
    driving_force, stiffness, coupling, friction, edge_coef, neighbours,
    send_cells, row_owner, pixel_cell, observed, look_vector,
):
    n = lax.axis_size("dom")
    cells = driving_force.shape[1]
    halo = send_cells.shape[1]
    ext = cells + 4 * halo
    here = pl.BlockSpec(memory_space=pltpu.HBM)
    rows, pixels = pixel_cell.shape
    vel, adj, lf = pl.pallas_call(
        body,
        out_shape=(
            jax.ShapeDtypeStruct(driving_force.shape, f32),
            jax.ShapeDtypeStruct(driving_force.shape, f32),
            jax.ShapeDtypeStruct((1, cells), f32),
        ),
        in_specs=[here] * 11,
        out_specs=(here, here, here),
        scratch_shapes=[
            pltpu.VMEM(driving_force.shape, f32),
            pltpu.VMEM((1, cells), f32),
            pltpu.VMEM((1, cells), f32),
            pltpu.VMEM((1, cells), f32),
            pltpu.VMEM(edge_coef.shape, f32),
            pltpu.VMEM(neighbours.shape, jnp.int32),
            pltpu.VMEM(send_cells.shape, jnp.int32),
            pltpu.VMEM((1, rows), jnp.int32),
            pltpu.VMEM((rows, pixels), jnp.int32),
            pltpu.VMEM((rows, pixels), f32),
            pltpu.VMEM((2, rows, pixels), f32),
            pltpu.VMEM(driving_force.shape, f32),
            pltpu.VMEM(driving_force.shape, f32),
            pltpu.VMEM((1, cells), f32),
            pltpu.VMEM((ext, cells), bf16),
            pltpu.VMEM((ext, cells), bf16),
            pltpu.VMEM((cells, 4 * halo), bf16),
            pltpu.VMEM((cells, 4 * halo), bf16),
            pltpu.VMEM((cells, 4 * halo), bf16),
            pltpu.VMEM((4 * halo, cells), bf16),
            pltpu.VMEM((16, cells), f32),
            pltpu.VMEM((8, cells), f32),
            pltpu.VMEM((8, cells), f32),
            pltpu.VMEM((n, 8, 128), f32),
            pltpu.VMEM((n, 8, 128), f32),
            pltpu.VMEM((ROUNDS, 4, 16, halo), f32),
            pltpu.VMEM((ROUNDS, 4, 16, halo), f32),
            pltpu.SemaphoreType.DMA((ROUNDS, 4)),
            pltpu.SemaphoreType.DMA((ROUNDS, 4)),
            pltpu.SemaphoreType.DMA((1,)),
            pltpu.SemaphoreType.DMA((1,)),
            pltpu.SemaphoreType.DMA((4,)),
            pltpu.SemaphoreType.DMA((7,)),
            pltpu.SemaphoreType.DMA((7,)),
            pltpu.SemaphoreType.DMA((3,)),
            pltpu.SemaphoreType.DMA((3,)),
        ],
        compiler_params=pltpu.CompilerParams(
            collective_id=0, has_side_effects=True, vmem_limit_bytes=62 * 1024 * 1024
        ),
    )(
        driving_force, stiffness[None, :], coupling[None, :], friction[None, :],
        edge_coef, neighbours, send_cells, row_owner.reshape(1, rows), pixel_cell,
        observed, look_vector,
    )
    return vel, adj, lf[0]


def solution(mesh):
    in_specs = (
        P(None, "dom"), P("dom"), P("dom"), P("dom"), P(None, "dom"), P(None, "dom"),
        P("dom", None), P("dom", None), P("dom", None), P("dom", None), P(None, "dom", None),
    )
    out_specs = (P(None, "dom"), P(None, "dom"), P("dom"))
    return jax.shard_map(local, mesh=mesh, in_specs=in_specs, out_specs=out_specs, check_vma=False)
```

```python
import jax
import jax.numpy as jnp
from jax import lax
from jax.experimental import pallas as pl
from jax.experimental.pallas import tpu as pltpu
from jax.sharding import PartitionSpec as P

SWEEPS = 4
STEPS = 2
OFFSETS = (1, -1, 2, -2)
ORDER = (2, 3, 0, 1)
RATE = 0.5
LAYERS = 5
ROUNDS = 13
MESH = pl.DeviceIdType.MESH
NT = (((1,), (1,)), ((), ()))
NN = (((1,), (0,)), ((), ()))
f32 = jnp.float32
bf16 = jnp.bfloat16


def split(x):
    hi = x.astype(bf16).astype(f32)
    return hi, x - hi


def stacked(x):
    hi, lo = split(x)
    return jnp.concatenate([hi, lo], axis=0).astype(bf16)


def mm(a, b, dims=NN):
    return lax.dot_general(a, b, dims, preferred_element_type=f32)


def iota(shape, dim):
    return lax.broadcasted_iota(jnp.int32, shape, dim)


def place_of(part):
    core = lax.rem(part, 2)
    chip = lax.div(part, 2)
    x = lax.rem(chip, 4)
    y = lax.rem(lax.div(chip, 4), 4)
    z = lax.div(chip, 16)
    x = x + lax.rem(y, 2) * (3 - 2 * x)
    y = y + lax.rem(z, 2) * (3 - 2 * y)
    return ((z * 4 + y) * 4 + x) * 2 + 1 - core


def part_at(device):
    core = lax.rem(device, 2)
    chip = lax.div(device, 2)
    x = lax.rem(chip, 4)
    y = lax.rem(lax.div(chip, 4), 4)
    z = lax.div(chip, 16)
    y = y + lax.rem(z, 2) * (3 - 2 * y)
    x = x + lax.rem(y, 2) * (3 - 2 * x)
    return ((z * 4 + y) * 4 + x) * 2 + 1 - core


def body(
    drv_in, stiff_in, coup_in, fric_in, edge_in, nbr_in, send_in,
    owner_in, pcell_in, obs_in, look_in,
    vel_out, adj_out, lf_out,
    drv, stiff, coup, fric, edge, nbr, send, owner, pcell, obs, look,
    vel, adjoint, logf,
    mhi, mlo, thi, tlo, sel, selt, frc, wts, sums, out, got, snd, rcv,
    ssem, rsem, asem, gsem, lsem, msem, isem, osem, hsem, ysem, zsem,
):
    n = lax.axis_size("dom")
    me = lax.axis_index("dom")
    mine = part_at(me)
    away = place_of(me)
    cells = drv.shape[1]
    halo = send.shape[1]
    ext = cells + 4 * halo

    loads = [
        pltpu.make_async_copy(src, dst, lsem.at[k])
        for k, (src, dst) in enumerate(
            [(owner_in, owner), (pcell_in, pcell), (obs_in, obs), (look_in, look)]
        )
    ]
    for c in loads:
        c.start()
    moves = [
        pltpu.make_async_remote_copy(
            src, dst, msem.at[k], isem.at[k], device_id=(away,), device_id_type=MESH
        )
        for k, (src, dst) in enumerate(
            [
                (send_in, send), (nbr_in, nbr), (edge_in, edge), (stiff_in, stiff),
                (coup_in, coup), (fric_in, fric), (drv_in, drv),
            ]
        )
    ]
    partners = [
        [place_of(lax.rem(mine + sign * o + n, n)) for o in OFFSETS] for sign in (1, -1)
    ]

    barrier = pltpu.get_barrier_semaphore()

    line = lax.div(me, 8) * 8
    y_mates = [lax.div(me, 32) * 32 + lax.rem(me + 8 * k, 32) for k in (1, 2, 3)]
    z_mates = [lax.rem(me + 32 * k, n) for k in (1, 2, 3)]
    near = [line + lax.rem(me + k, 8) for k in range(1, 8)]
    near += y_mates + z_mates + partners[0] + [away, mine]
    for peer in near:
        pl.semaphore_signal(barrier, inc=1, device_id=(peer,), device_id_type=MESH)

    pl.semaphore_wait(barrier, len(near))
    for c in moves:
        c.start()
    for peer in y_mates:
        pl.semaphore_signal(ysem, inc=1, device_id=(peer,), device_id_type=MESH)

    for c in loads:
        c.wait()
    own_row = owner[...].astype(f32)
    eye = iota((128, 128), 0) == iota((128, 128), 1)
    own_col = jnp.sum(jnp.where(eye, own_row, 0.0), axis=1, keepdims=True)
    before = (own_col == own_row) & (iota((128, 128), 0) < iota((128, 128), 1))
    rank = jnp.sum(jnp.where(before, 1.0, 0.0), axis=0, keepdims=True)
    first_line = place_of(owner[...]) * 8 + rank.astype(jnp.int32)
    lines = jnp.concatenate([first_line + 2 * q for q in range(4)], axis=1)
    data = jnp.concatenate(
        [pcell[...].astype(f32), obs[...], look[0], look[1]], axis=0
    )
    hi, lo = split(data)
    data = jnp.concatenate([hi, lo], axis=1).astype(bf16)
    for b in range(8):
        hit = iota((128, 512), 0) + 128 * b == lines
        placed = mm(jnp.where(hit, 1.0, 0.0).astype(bf16), data)
        placed = placed[:, 0:128] + placed[:, 128:256]
        out[b * 16 : (b + 1) * 16] = placed.reshape(16, 8, 128)

    pl.semaphore_wait(ysem, 3)
    for peer in z_mates:
        pl.semaphore_signal(zsem, inc=1, device_id=(peer,), device_id_type=MESH)
    def row_copy(r):
        peer = lax.rem(me + r, n)
        return pltpu.make_async_remote_copy(
            out.at[peer], got.at[me], asem.at[0], gsem.at[0],
            device_id=(peer,), device_id_type=MESH,
        )

    def row_start(r, carry):
        row_copy(r).start()
        return carry

    got[me] = out[me]
    pl.semaphore_wait(zsem, 3)
    lax.fori_loop(1, n, row_start, 0)
    for c in moves:
        c.wait_recv()

    weights = jnp.where(nbr[...] != iota((8, cells), 1), edge[...], 0.0)
    wts[...] = weights
    rowsum = jnp.sum(weights, axis=0, keepdims=True)
    layer = iota((8, cells), 0)
    links = jnp.where((layer == 0) | (layer == LAYERS - 1), 1.0, 2.0)
    coupling = coup[...]
    static_diag = stiff[...] + rowsum + coupling * links

    frc[...] = jnp.zeros_like(frc)
    frc[0:LAYERS, :] = drv[0:LAYERS, :]
    frc[8 : 8 + LAYERS, :] = drv[LAYERS : 2 * LAYERS, :]

    def inverse(lf):
        diag = static_diag + jnp.where(layer == LAYERS - 1, jnp.exp(lf), 0.0)
        return jnp.where(layer < LAYERS, 1.0 / diag, 0.0)

    def scaled(x, inv):
        return jnp.concatenate([x[0:8] * inv, x[8:16] * inv], axis=0)

    def vertical(x):
        return coupling * (pltpu.roll(x, 1, 0) + pltpu.roll(x, 15, 0))

    for j in range(4):
        hit = iota((cells, halo), 0) == send[j : j + 1, :]
        sel[:, j * halo : (j + 1) * halo] = jnp.where(hit, 1.0, 0.0).astype(bf16)

    name = nbr[...]
    total = weights
    again = jnp.zeros(name.shape, jnp.int32)
    for shift in range(1, 8):
        same = pltpu.roll(name, shift, 0) == name
        total = total + jnp.where(same, pltpu.roll(weights, shift, 0), 0.0)
        again = again + jnp.where(same & (layer >= shift), 1, 0)
    name = jnp.where(again > 0, -1, name).astype(jnp.int16)
    part_hi, part_lo = split(total)
    part_hi = part_hi.astype(bf16)
    part_lo = part_lo.astype(bf16)

    def build():
        width = 256
        for c in range(0, cells, width):
            def line_of(a, e):
                return jnp.broadcast_to(a[e : e + 1, c : c + width], (16, width))

            names = [line_of(name, e) for e in range(8)]
            his = [line_of(part_hi, e) for e in range(8)]
            los = [line_of(part_lo, e) for e in range(8)]

            def rows_of(b, carry):
                base = pl.multiple_of(b * 16, 16)
                rows = (iota((16, width), 0) + base).astype(jnp.int16)
                hi = jnp.zeros((16, width), bf16)
                lo = jnp.zeros((16, width), bf16)
                for e in range(8):
                    hit = rows == names[e]
                    hi = jnp.where(hit, his[e], hi)
                    lo = jnp.where(hit, los[e], lo)
                mhi[pl.ds(base, 16), c : c + width] = hi
                mlo[pl.ds(base, 16), c : c + width] = lo
                return carry

            lax.fori_loop(0, ext // 16, rows_of, 0, unroll=8)

    def rows_done(sem, ref):
        all_but_one = ref.at[pl.ds(0, n - 1)]
        pltpu.make_async_copy(all_but_one, all_but_one, sem.at[0]).wait()

    def pixels(g, acc):
        lhs = []
        rhs = []
        for s in range(16):
            blk = got[g * 16 + s]
            for slot in range(2):
                idx = blk[slot : slot + 1].astype(jnp.int32)
                ob = blk[2 + slot : 3 + slot]
                lx = blk[4 + slot : 5 + slot]
                ly = blk[6 + slot : 7 + slot]
                low = jnp.broadcast_to((idx & 127).astype(jnp.int16), (128, 128))
                low = iota((128, 128), 0).astype(jnp.int16) == low
                rhs.append(jnp.where(low, jnp.ones_like(low, bf16), jnp.zeros_like(low, bf16)))
                high = iota((8, 128), 0) == (idx >> 7)
                vals = [
                    jnp.where(high, q, 0.0)
                    for q in (lx * lx, lx * ly, ly * ly, lx * ob, ly * ob)
                ]
                lhs.append(stacked(jnp.concatenate(vals, axis=0)))
        return acc + mm(jnp.concatenate(lhs, axis=1), jnp.concatenate(rhs, axis=1), NT)

    def copies(i, sign):
        return [
            pltpu.make_async_remote_copy(
                snd.at[i, j],
                rcv.at[i, j],
                ssem.at[i, j],
                rsem.at[i, j],
                device_id=(partners[0 if sign == 1 else 1][j],),
                device_id_type=MESH,
            )
            for j in range(4)
        ]

    def push(i, piece, sign):
        cps = copies(i, sign)
        for j in ORDER:
            snd[i, j] = piece[:, j * halo : (j + 1) * halo]
            cps[j].start()

    def fetched(i, sign):
        for c in copies(i, sign):
            c.wait_recv()
        return stacked(jnp.concatenate([rcv[i, j] for j in range(4)], axis=1))

    def two(xs, hi, lo, dims=NN):
        a = mm(xs, hi, dims)
        return a[0:16] + a[16:32] + mm(xs[0:16], lo, dims)

    def fwd_send(i, xs):
        piece = mm(xs, sel[...])
        push(i, piece[0:16] + piece[16:32], 1)

    def fwd_own(xs):
        return two(xs, mhi[0:cells, :], mlo[0:cells, :])

    def fwd_halo(i):
        return two(fetched(i, 1), mhi[cells:ext, :], mlo[cells:ext, :])

    def fwd(i, x, inv, extra=None):
        xs = stacked(x)
        fwd_send(i, xs)
        if extra is not None:
            extra()
        own = fwd_own(xs) + frc[...] + vertical(x)
        return scaled(own + fwd_halo(i), inv)

    def adj(i, x, source, inv, extra=None):
        xs = stacked(x)
        push(i, two(xs, thi[...], tlo[...]), -1)
        if extra is not None:
            extra()
        own = two(xs, mhi[0:cells, :], mlo[0:cells, :], NT) + source + vertical(x)
        a = mm(fetched(i, -1), selt[...])
        return scaled(own + a[0:16] + a[16:32], inv)

    lf = jnp.log(fric[...])
    inv = inverse(lf)
    x = scaled(frc[...], inv)

    def during_first():
        build()

    halves = []

    def during_second():
        thi[...] = mhi[cells:ext, :].astype(f32).T.astype(bf16)
        tlo[...] = mlo[cells:ext, :].astype(f32).T.astype(bf16)
        rows_done(gsem, got)
        halves.append(lax.fori_loop(0, n // 32, pixels, jnp.zeros((80, 128), f32)))

    def during_third():
        acc = lax.fori_loop(n // 32, n // 16, pixels, halves[0])
        tot = acc[0:40] + acc[40:80]
        for q in range(5):
            for h in range(8):
                line = q * 8 + h
                sums[q : q + 1, h * 128 : (h + 1) * 128] = tot[line : line + 1]

    x = fwd(0, x, inv, during_first)
    x = fwd(1, x, inv, during_second)
    x = fwd(2, x, inv, during_third)

    def source_of(x):
        mx = jnp.sum(x[0:8], axis=0, keepdims=True) / LAYERS
        my = jnp.sum(x[8:16], axis=0, keepdims=True) / LAYERS
        px = (sums[0:1, :] * mx + sums[1:2, :] * my - sums[3:4, :]) / LAYERS
        py = (sums[1:2, :] * mx + sums[2:3, :] * my - sums[4:5, :]) / LAYERS
        return jnp.concatenate(
            [jnp.broadcast_to(px, (8, cells)), jnp.broadcast_to(py, (8, cells))], axis=0
        )

    def stepped(lf, lam, x):
        grad = -(lam[4:5] * x[4:5] + lam[12:13] * x[12:13])
        return lf - RATE * jnp.tanh(jnp.exp(lf) * grad)

    homeward = [
        pltpu.make_async_remote_copy(
            src, dst, osem.at[k], hsem.at[k], device_id=(mine,), device_id_type=MESH
        )
        for k, (src, dst) in enumerate([(vel, vel_out), (adjoint, adj_out), (logf, lf_out)])
    ]

    source = source_of(x)
    lam = scaled(source, inv)
    held = []

    def early_send():
        selt[...] = sel[...].astype(f32).T.astype(bf16)
        fwd_send(6, stacked(x))

    def early_across():
        held.append(fwd_own(stacked(x)) + fwd_halo(6) + frc[...] + vertical(x))

    lam = adj(3, lam, source, inv, early_send)
    lam = adj(4, lam, source, inv, early_across)
    lam = adj(5, lam, source, inv)
    lf = stepped(lf, lam, x)

    inv = inverse(lf)
    x = scaled(held[0], inv)
    x = lax.fori_loop(7, 10, lambda i, v: fwd(i, v, inv), x)
    source = source_of(x)
    lam = scaled(source, inv)
    vel[0:LAYERS, :] = x[0:LAYERS]
    vel[LAYERS : 2 * LAYERS, :] = x[8 : 8 + LAYERS]
    homeward[0].start()
    lam = lax.fori_loop(10, 13, lambda i, v: adj(i, v, source, inv), lam)
    lf = stepped(lf, lam, x)

    adjoint[0:LAYERS, :] = lam[0:LAYERS]
    adjoint[LAYERS : 2 * LAYERS, :] = lam[8 : 8 + LAYERS]
    homeward[1].start()
    logf[...] = lf
    homeward[2].start()

    def drain(i, carry):
        for c in copies(i, 1):
            c.wait_send()
        return carry

    lax.fori_loop(0, ROUNDS, drain, 0)
    rows_done(asem, out)
    for c in moves:
        c.wait_send()
    for c in homeward:
        c.wait()


def local(
    driving_force, stiffness, coupling, friction, edge_coef, neighbours,
    send_cells, row_owner, pixel_cell, observed, look_vector,
):
    n = lax.axis_size("dom")
    cells = driving_force.shape[1]
    halo = send_cells.shape[1]
    ext = cells + 4 * halo
    here = pl.BlockSpec(memory_space=pltpu.HBM)
    vmem = pl.BlockSpec(memory_space=pltpu.VMEM)
    rows, pixels = pixel_cell.shape
    results = (
        jax.ShapeDtypeStruct(driving_force.shape, f32),
        jax.ShapeDtypeStruct(driving_force.shape, f32),
        jax.ShapeDtypeStruct((1, cells), f32),
    )
    vel, adj, lf = pl.pallas_call(
        body,
        out_shape=results,
        in_specs=[here] * 11,
        out_specs=(vmem, vmem, vmem),
        scratch_shapes=[
            pltpu.VMEM(driving_force.shape, f32),
            pltpu.VMEM((1, cells), f32),
            pltpu.VMEM((1, cells), f32),
            pltpu.VMEM((1, cells), f32),
            pltpu.VMEM(edge_coef.shape, f32),
            pltpu.VMEM(neighbours.shape, jnp.int32),
            pltpu.VMEM(send_cells.shape, jnp.int32),
            pltpu.VMEM((1, rows), jnp.int32),
            pltpu.VMEM((rows, pixels), jnp.int32),
            pltpu.VMEM((rows, pixels), f32),
            pltpu.VMEM((2, rows, pixels), f32),
            pltpu.VMEM(driving_force.shape, f32),
            pltpu.VMEM(driving_force.shape, f32),
            pltpu.VMEM((1, cells), f32),
            pltpu.VMEM((ext, cells), bf16),
            pltpu.VMEM((ext, cells), bf16),
            pltpu.VMEM((cells, 4 * halo), bf16),
            pltpu.VMEM((cells, 4 * halo), bf16),
            pltpu.VMEM((cells, 4 * halo), bf16),
            pltpu.VMEM((4 * halo, cells), bf16),
            pltpu.VMEM((16, cells), f32),
            pltpu.VMEM((8, cells), f32),
            pltpu.VMEM((8, cells), f32),
            pltpu.VMEM((n, 8, 128), f32),
            pltpu.VMEM((n, 8, 128), f32),
            pltpu.VMEM((ROUNDS, 4, 16, halo), f32),
            pltpu.VMEM((ROUNDS, 4, 16, halo), f32),
            pltpu.SemaphoreType.DMA((ROUNDS, 4)),
            pltpu.SemaphoreType.DMA((ROUNDS, 4)),
            pltpu.SemaphoreType.DMA((1,)),
            pltpu.SemaphoreType.DMA((1,)),
            pltpu.SemaphoreType.DMA((4,)),
            pltpu.SemaphoreType.DMA((7,)),
            pltpu.SemaphoreType.DMA((7,)),
            pltpu.SemaphoreType.DMA((3,)),
            pltpu.SemaphoreType.DMA((3,)),
            pltpu.SemaphoreType.REGULAR,
            pltpu.SemaphoreType.REGULAR,
        ],
        compiler_params=pltpu.CompilerParams(
            collective_id=0, has_side_effects=True, vmem_limit_bytes=48 * 1024 * 1024
        ),
    )(*[
        pltpu.with_memory_space_constraint(a, pltpu.HBM)
        for a in (
            driving_force, stiffness[None, :], coupling[None, :], friction[None, :],
            edge_coef, neighbours, send_cells, row_owner.reshape(1, rows), pixel_cell,
            observed, look_vector,
        )
    ])
    return vel, adj, lf[0]


def solution(mesh):
    in_specs = (
        P(None, "dom"), P("dom"), P("dom"), P("dom"), P(None, "dom"), P(None, "dom"),
        P("dom", None), P("dom", None), P("dom", None), P("dom", None), P(None, "dom", None),
    )
    out_specs = (P(None, "dom"), P(None, "dom"), P("dom"))
    return jax.shard_map(local, mesh=mesh, in_specs=in_specs, out_specs=out_specs, check_vma=False)
```

```python
import jax
import jax.numpy as jnp
from jax import lax
from jax.experimental import pallas as pl
from jax.experimental.pallas import tpu as pltpu
from jax.sharding import PartitionSpec as P

SWEEPS = 4
STEPS = 2
OFFSETS = (1, -1, 2, -2)
ORDER = (2, 3, 0, 1)
RATE = 0.5
LAYERS = 5
ROUNDS = 13
MESH = pl.DeviceIdType.MESH
NT = (((1,), (1,)), ((), ()))
NN = (((1,), (0,)), ((), ()))
f32 = jnp.float32
bf16 = jnp.bfloat16


def split(x):
    hi = x.astype(bf16).astype(f32)
    return hi, x - hi


def stacked(x):
    hi, lo = split(x)
    return jnp.concatenate([hi, lo], axis=0).astype(bf16)


def mm(a, b, dims=NN):
    return lax.dot_general(a, b, dims, preferred_element_type=f32)


def iota(shape, dim):
    return lax.broadcasted_iota(jnp.int32, shape, dim)


def place_of(part):
    core = lax.rem(part, 2)
    chip = lax.div(part, 2)
    x = lax.rem(chip, 4)
    y = lax.rem(lax.div(chip, 4), 4)
    z = lax.div(chip, 16)
    x = x + lax.rem(y, 2) * (3 - 2 * x)
    y = y + lax.rem(z, 2) * (3 - 2 * y)
    return ((z * 4 + y) * 4 + x) * 2 + 1 - core


def part_at(device):
    core = lax.rem(device, 2)
    chip = lax.div(device, 2)
    x = lax.rem(chip, 4)
    y = lax.rem(lax.div(chip, 4), 4)
    z = lax.div(chip, 16)
    y = y + lax.rem(z, 2) * (3 - 2 * y)
    x = x + lax.rem(y, 2) * (3 - 2 * x)
    return ((z * 4 + y) * 4 + x) * 2 + 1 - core


def body(
    drv_in, stiff_in, coup_in, fric_in, edge_in, nbr_in, send_in,
    owner_in, pcell_in, obs_in, look_in,
    vel_out, adj_out, lf_out,
    drv, stiff, coup, fric, edge, nbr, send, owner, pcell, obs, look,
    vel, adjoint, logf,
    mhi, mlo, thi, tlo, sel, selt, frc, wts, sums, out, got, snd, rcv,
    ssem, rsem, asem, gsem, lsem, msem, isem, osem, hsem, ysem, zsem,
):
    n = lax.axis_size("dom")
    me = lax.axis_index("dom")
    mine = part_at(me)
    away = place_of(me)
    cells = drv.shape[1]
    halo = send.shape[1]
    ext = cells + 4 * halo

    loads = [
        pltpu.make_async_copy(src, dst, lsem.at[k])
        for k, (src, dst) in enumerate(
            [(owner_in, owner), (pcell_in, pcell), (obs_in, obs), (look_in, look)]
        )
    ]
    for c in loads:
        c.start()
    moves = [
        pltpu.make_async_remote_copy(
            src, dst, msem.at[k], isem.at[k], device_id=(away,), device_id_type=MESH
        )
        for k, (src, dst) in enumerate(
            [
                (send_in, send), (nbr_in, nbr), (edge_in, edge), (stiff_in, stiff),
                (coup_in, coup), (fric_in, fric), (drv_in, drv),
            ]
        )
    ]
    partners = [
        [place_of(lax.rem(mine + sign * o + n, n)) for o in OFFSETS] for sign in (1, -1)
    ]

    barrier = pltpu.get_barrier_semaphore()

    line = lax.div(me, 8) * 8
    y_mates = [lax.div(me, 32) * 32 + lax.rem(me + 8 * k, 32) for k in (1, 2, 3)]
    z_mates = [lax.rem(me + 32 * k, n) for k in (1, 2, 3)]
    near = [line + lax.rem(me + k, 8) for k in range(1, 8)]
    near += y_mates + z_mates + partners[0] + [away, mine]
    for peer in near:
        pl.semaphore_signal(barrier, inc=1, device_id=(peer,), device_id_type=MESH)

    pl.semaphore_wait(barrier, len(near))
    for c in moves:
        c.start()
    for peer in y_mates:
        pl.semaphore_signal(ysem, inc=1, device_id=(peer,), device_id_type=MESH)

    for c in loads:
        c.wait()
    own_row = owner[...].astype(f32)
    eye = iota((128, 128), 0) == iota((128, 128), 1)
    own_col = jnp.sum(jnp.where(eye, own_row, 0.0), axis=1, keepdims=True)
    before = (own_col == own_row) & (iota((128, 128), 0) < iota((128, 128), 1))
    rank = jnp.sum(jnp.where(before, 1.0, 0.0), axis=0, keepdims=True)
    first_line = place_of(owner[...]) * 8 + rank.astype(jnp.int32)
    lines = jnp.concatenate([first_line + 2 * q for q in range(4)], axis=1)
    data = jnp.concatenate(
        [pcell[...].astype(f32), obs[...], look[0], look[1]], axis=0
    )
    hi, lo = split(data)
    data = jnp.concatenate([hi, lo], axis=1).astype(bf16)
    for b in range(8):
        hit = iota((128, 512), 0) + 128 * b == lines
        placed = mm(jnp.where(hit, 1.0, 0.0).astype(bf16), data)
        placed = placed[:, 0:128] + placed[:, 128:256]
        out[b * 16 : (b + 1) * 16] = placed.reshape(16, 8, 128)

    pl.semaphore_wait(ysem, 3)
    for peer in z_mates:
        pl.semaphore_signal(zsem, inc=1, device_id=(peer,), device_id_type=MESH)
    def row_copy(r):
        peer = lax.rem(me + r, n)
        return pltpu.make_async_remote_copy(
            out.at[peer], got.at[me], asem.at[0], gsem.at[0],
            device_id=(peer,), device_id_type=MESH,
        )

    def row_starts(b, carry):
        for k in range(9):
            row_copy(b * 9 + 1 + k).start()
        return carry

    got[me] = out[me]
    pl.semaphore_wait(zsem, 3)
    lax.fori_loop(0, (n - 2) // 9, row_starts, 0)
    row_copy(n - 1).start()

    moves[0].wait_recv()
    for j in range(4):
        hit = iota((cells, halo), 0) == send[j : j + 1, :]
        sel[:, j * halo : (j + 1) * halo] = jnp.where(hit, 1.0, 0.0).astype(bf16)
    for c in moves[1:]:
        c.wait_recv()

    weights = jnp.where(nbr[...] != iota((8, cells), 1), edge[...], 0.0)
    wts[...] = weights
    rowsum = jnp.sum(weights, axis=0, keepdims=True)
    layer = iota((8, cells), 0)
    links = jnp.where((layer == 0) | (layer == LAYERS - 1), 1.0, 2.0)
    coupling = coup[...]
    static_diag = stiff[...] + rowsum + coupling * links

    frc[...] = jnp.zeros_like(frc)
    frc[0:LAYERS, :] = drv[0:LAYERS, :]
    frc[8 : 8 + LAYERS, :] = drv[LAYERS : 2 * LAYERS, :]

    def inverse(lf):
        diag = static_diag + jnp.where(layer == LAYERS - 1, jnp.exp(lf), 0.0)
        return jnp.where(layer < LAYERS, 1.0 / diag, 0.0)

    def scaled(x, inv):
        return jnp.concatenate([x[0:8] * inv, x[8:16] * inv], axis=0)

    def vertical(x):
        return coupling * (pltpu.roll(x, 1, 0) + pltpu.roll(x, 15, 0))

    def build():
        name = nbr[...]
        total = weights
        again = jnp.zeros(name.shape, jnp.int32)
        for shift in range(1, 8):
            same = pltpu.roll(name, shift, 0) == name
            total = total + jnp.where(same, pltpu.roll(weights, shift, 0), 0.0)
            again = again + jnp.where(same & (layer >= shift), 1, 0)
        name = jnp.where(again > 0, -1, name).astype(jnp.int16)
        part_hi, part_lo = split(total)
        part_hi = part_hi.astype(bf16)
        part_lo = part_lo.astype(bf16)
        width = 256
        for c in range(0, cells, width):
            def line_of(a, e):
                return jnp.broadcast_to(a[e : e + 1, c : c + width], (16, width))

            names = [line_of(name, e) for e in range(8)]
            his = [line_of(part_hi, e) for e in range(8)]
            los = [line_of(part_lo, e) for e in range(8)]

            def rows_of(b, carry):
                base = pl.multiple_of(b * 16, 16)
                rows = (iota((16, width), 0) + base).astype(jnp.int16)
                hi = jnp.zeros((16, width), bf16)
                lo = jnp.zeros((16, width), bf16)
                for e in range(8):
                    hit = rows == names[e]
                    hi = jnp.where(hit, his[e], hi)
                    lo = jnp.where(hit, los[e], lo)
                mhi[pl.ds(base, 16), c : c + width] = hi
                mlo[pl.ds(base, 16), c : c + width] = lo
                return carry

            lax.fori_loop(0, ext // 16, rows_of, 0, unroll=8)

    def rows_done(sem, ref):
        all_but_one = ref.at[pl.ds(0, n - 1)]
        pltpu.make_async_copy(all_but_one, all_but_one, sem.at[0]).wait()

    def pixels(g, acc):
        lhs = []
        rhs = []
        for s in range(16):
            blk = got[g * 16 + s]
            for slot in range(2):
                idx = blk[slot : slot + 1].astype(jnp.int32)
                ob = blk[2 + slot : 3 + slot]
                lx = blk[4 + slot : 5 + slot]
                ly = blk[6 + slot : 7 + slot]
                low = jnp.broadcast_to((idx & 127).astype(jnp.int16), (128, 128))
                low = iota((128, 128), 0).astype(jnp.int16) == low
                rhs.append(jnp.where(low, jnp.ones_like(low, bf16), jnp.zeros_like(low, bf16)))
                high = iota((8, 128), 0) == (idx >> 7)
                vals = [
                    jnp.where(high, q, 0.0)
                    for q in (lx * lx, lx * ly, ly * ly, lx * ob, ly * ob)
                ]
                lhs.append(stacked(jnp.concatenate(vals, axis=0)))
        return acc + mm(jnp.concatenate(lhs, axis=1), jnp.concatenate(rhs, axis=1), NT)

    def copies(i, sign):
        return [
            pltpu.make_async_remote_copy(
                snd.at[i, j],
                rcv.at[i, j],
                ssem.at[i],
                rsem.at[i],
                device_id=(partners[0 if sign == 1 else 1][j],),
                device_id_type=MESH,
            )
            for j in range(4)
        ]

    def push(i, piece, sign):
        cps = copies(i, sign)
        for j in ORDER:
            snd[i, j] = piece[:, j * halo : (j + 1) * halo]
            cps[j].start()

    def fetched(i):
        pltpu.make_async_copy(rcv.at[i], rcv.at[i], rsem.at[i]).wait()
        return stacked(jnp.concatenate([rcv[i, j] for j in range(4)], axis=1))

    def two(xs, hi, lo, dims=NN):
        a = mm(xs, hi, dims)
        return a[0:16] + a[16:32] + mm(xs[0:16], lo, dims)

    def fwd_send(i, xs):
        piece = mm(xs, sel[...])
        push(i, piece[0:16] + piece[16:32], 1)

    def fwd_own(xs):
        return two(xs, mhi[0:cells, :], mlo[0:cells, :])

    def fwd_halo(i):
        return two(fetched(i), mhi[cells:ext, :], mlo[cells:ext, :])

    def fwd(i, x, inv, extra=None):
        xs = stacked(x)
        fwd_send(i, xs)
        if extra is not None:
            extra()
        own = fwd_own(xs) + frc[...] + vertical(x)
        return scaled(own + fwd_halo(i), inv)

    def adj(i, x, source, inv, extra=None):
        xs = stacked(x)
        push(i, two(xs, thi[...], tlo[...]), -1)
        if extra is not None:
            extra()
        own = two(xs, mhi[0:cells, :], mlo[0:cells, :], NT) + source + vertical(x)
        a = mm(fetched(i), selt[...])
        return scaled(own + a[0:16] + a[16:32], inv)

    lf = jnp.log(fric[...])
    inv = inverse(lf)
    x = scaled(frc[...], inv)

    def during_first():
        build()

    halves = []

    def during_second():
        thi[...] = mhi[cells:ext, :].astype(f32).T.astype(bf16)
        tlo[...] = mlo[cells:ext, :].astype(f32).T.astype(bf16)
        rows_done(gsem, got)
        halves.append(lax.fori_loop(0, n // 32, pixels, jnp.zeros((80, 128), f32)))

    def during_third():
        acc = lax.fori_loop(n // 32, n // 16, pixels, halves[0])
        tot = acc[0:40] + acc[40:80]
        for q in range(5):
            for h in range(8):
                line = q * 8 + h
                sums[q : q + 1, h * 128 : (h + 1) * 128] = tot[line : line + 1]

    x = fwd(0, x, inv, during_first)
    x = fwd(1, x, inv, during_second)
    x = fwd(2, x, inv, during_third)

    def source_of(x):
        mx = jnp.sum(x[0:8], axis=0, keepdims=True) / LAYERS
        my = jnp.sum(x[8:16], axis=0, keepdims=True) / LAYERS
        px = (sums[0:1, :] * mx + sums[1:2, :] * my - sums[3:4, :]) / LAYERS
        py = (sums[1:2, :] * mx + sums[2:3, :] * my - sums[4:5, :]) / LAYERS
        return jnp.concatenate(
            [jnp.broadcast_to(px, (8, cells)), jnp.broadcast_to(py, (8, cells))], axis=0
        )

    def stepped(lf, lam, x):
        grad = -(lam[4:5] * x[4:5] + lam[12:13] * x[12:13])
        return lf - RATE * jnp.tanh(jnp.exp(lf) * grad)

    homeward = [
        pltpu.make_async_remote_copy(
            src, dst, osem.at[k], hsem.at[k], device_id=(mine,), device_id_type=MESH
        )
        for k, (src, dst) in enumerate([(vel, vel_out), (adjoint, adj_out), (logf, lf_out)])
    ]

    source = source_of(x)
    lam = scaled(source, inv)
    held = []

    def early_send():
        selt[...] = sel[...].astype(f32).T.astype(bf16)
        fwd_send(6, stacked(x))

    def early_across():
        held.append(fwd_own(stacked(x)) + fwd_halo(6) + frc[...] + vertical(x))

    lam = adj(3, lam, source, inv, early_send)
    lam = adj(4, lam, source, inv, early_across)
    lam = adj(5, lam, source, inv)
    lf = stepped(lf, lam, x)

    inv = inverse(lf)
    x = scaled(held[0], inv)
    x = lax.fori_loop(7, 10, lambda i, v: fwd(i, v, inv), x)
    source = source_of(x)
    lam = scaled(source, inv)
    vel[0:LAYERS, :] = x[0:LAYERS]
    vel[LAYERS : 2 * LAYERS, :] = x[8 : 8 + LAYERS]
    homeward[0].start()
    lam = lax.fori_loop(10, 13, lambda i, v: adj(i, v, source, inv), lam)
    lf = stepped(lf, lam, x)

    adjoint[0:LAYERS, :] = lam[0:LAYERS]
    adjoint[LAYERS : 2 * LAYERS, :] = lam[8 : 8 + LAYERS]
    homeward[1].start()
    logf[...] = lf
    homeward[2].start()

    def drain(i, carry):
        pltpu.make_async_copy(snd.at[i], snd.at[i], ssem.at[i]).wait()
        return carry

    lax.fori_loop(0, ROUNDS, drain, 0)
    rows_done(asem, out)
    for c in moves:
        c.wait_send()
    for c in homeward:
        c.wait()


def finish(vel_in, adj_in, lf_in, vel_out, adj_out, lf_out, sem):
    cps = [
        pltpu.make_async_copy(src, dst, sem.at[k])
        for k, (src, dst) in enumerate(
            [(vel_in, vel_out), (adj_in, adj_out), (lf_in, lf_out)]
        )
    ]
    for c in cps:
        c.start()
    for c in cps:
        c.wait()


def local(
    driving_force, stiffness, coupling, friction, edge_coef, neighbours,
    send_cells, row_owner, pixel_cell, observed, look_vector,
):
    n = lax.axis_size("dom")
    cells = driving_force.shape[1]
    halo = send_cells.shape[1]
    ext = cells + 4 * halo
    here = pl.BlockSpec(memory_space=pltpu.HBM)
    vmem = pl.BlockSpec(memory_space=pltpu.VMEM)
    rows, pixels = pixel_cell.shape
    results = (
        jax.ShapeDtypeStruct(driving_force.shape, f32),
        jax.ShapeDtypeStruct(driving_force.shape, f32),
        jax.ShapeDtypeStruct((1, cells), f32),
    )
    vel, adj, lf = pl.pallas_call(
        body,
        out_shape=results,
        in_specs=[here] * 11,
        out_specs=(vmem, vmem, vmem),
        scratch_shapes=[
            pltpu.VMEM(driving_force.shape, f32),
            pltpu.VMEM((1, cells), f32),
            pltpu.VMEM((1, cells), f32),
            pltpu.VMEM((1, cells), f32),
            pltpu.VMEM(edge_coef.shape, f32),
            pltpu.VMEM(neighbours.shape, jnp.int32),
            pltpu.VMEM(send_cells.shape, jnp.int32),
            pltpu.VMEM((1, rows), jnp.int32),
            pltpu.VMEM((rows, pixels), jnp.int32),
            pltpu.VMEM((rows, pixels), f32),
            pltpu.VMEM((2, rows, pixels), f32),
            pltpu.VMEM(driving_force.shape, f32),
            pltpu.VMEM(driving_force.shape, f32),
            pltpu.VMEM((1, cells), f32),
            pltpu.VMEM((ext, cells), bf16),
            pltpu.VMEM((ext, cells), bf16),
            pltpu.VMEM((cells, 4 * halo), bf16),
            pltpu.VMEM((cells, 4 * halo), bf16),
            pltpu.VMEM((cells, 4 * halo), bf16),
            pltpu.VMEM((4 * halo, cells), bf16),
            pltpu.VMEM((16, cells), f32),
            pltpu.VMEM((8, cells), f32),
            pltpu.VMEM((8, cells), f32),
            pltpu.VMEM((n, 8, 128), f32),
            pltpu.VMEM((n, 8, 128), f32),
            pltpu.VMEM((ROUNDS, 4, 16, halo), f32),
            pltpu.VMEM((ROUNDS, 4, 16, halo), f32),
            pltpu.SemaphoreType.DMA((ROUNDS,)),
            pltpu.SemaphoreType.DMA((ROUNDS,)),
            pltpu.SemaphoreType.DMA((1,)),
            pltpu.SemaphoreType.DMA((1,)),
            pltpu.SemaphoreType.DMA((4,)),
            pltpu.SemaphoreType.DMA((7,)),
            pltpu.SemaphoreType.DMA((7,)),
            pltpu.SemaphoreType.DMA((3,)),
            pltpu.SemaphoreType.DMA((3,)),
            pltpu.SemaphoreType.REGULAR,
            pltpu.SemaphoreType.REGULAR,
        ],
        compiler_params=pltpu.CompilerParams(
            collective_id=0, has_side_effects=True, vmem_limit_bytes=48 * 1024 * 1024
        ),
    )(*[
        pltpu.with_memory_space_constraint(a, pltpu.HBM)
        for a in (
            driving_force, stiffness[None, :], coupling[None, :], friction[None, :],
            edge_coef, neighbours, send_cells, row_owner.reshape(1, rows), pixel_cell,
            observed, look_vector,
        )
    ])
    vel, adj, lf = pl.pallas_call(
        finish,
        out_shape=results,
        in_specs=[vmem] * 3,
        out_specs=(here, here, here),
        scratch_shapes=[pltpu.SemaphoreType.DMA((3,))],
        compiler_params=pltpu.CompilerParams(vmem_limit_bytes=2 * 1024 * 1024),
    )(vel, adj, lf)
    return vel, adj, lf[0]


def solution(mesh):
    in_specs = (
        P(None, "dom"), P("dom"), P("dom"), P("dom"), P(None, "dom"), P(None, "dom"),
        P("dom", None), P("dom", None), P("dom", None), P("dom", None), P(None, "dom", None),
    )
    out_specs = (P(None, "dom"), P(None, "dom"), P("dom"))
    return jax.shard_map(local, mesh=mesh, in_specs=in_specs, out_specs=out_specs, check_vma=False)
```

```python
import jax
import jax.numpy as jnp
from jax import lax
from jax.experimental import pallas as pl
from jax.experimental.pallas import tpu as pltpu
from jax.sharding import PartitionSpec as P

SWEEPS = 4
STEPS = 2
OFFSETS = (1, -1, 2, -2)
ORDER = (2, 3, 0, 1)
RATE = 0.5
LAYERS = 5
ROUNDS = 12
MESH = pl.DeviceIdType.MESH
NT = (((1,), (1,)), ((), ()))
NN = (((1,), (0,)), ((), ()))
f32 = jnp.float32
bf16 = jnp.bfloat16


def split(x):
    hi = x.astype(bf16).astype(f32)
    return hi, x - hi


def stacked(x):
    hi, lo = split(x)
    return jnp.concatenate([hi, lo], axis=0).astype(bf16)


def mm(a, b, dims=NN):
    return lax.dot_general(a, b, dims, preferred_element_type=f32)


def iota(shape, dim):
    return lax.broadcasted_iota(jnp.int32, shape, dim)


def place_of(part):
    core = lax.rem(part, 2)
    chip = lax.div(part, 2)
    x = lax.rem(chip, 4)
    y = lax.rem(lax.div(chip, 4), 4)
    z = lax.div(chip, 16)
    x = x + lax.rem(y, 2) * (3 - 2 * x)
    y = y + lax.rem(z, 2) * (3 - 2 * y)
    return ((z * 4 + y) * 4 + x) * 2 + 1 - core


def part_at(device):
    core = lax.rem(device, 2)
    chip = lax.div(device, 2)
    x = lax.rem(chip, 4)
    y = lax.rem(lax.div(chip, 4), 4)
    z = lax.div(chip, 16)
    y = y + lax.rem(z, 2) * (3 - 2 * y)
    x = x + lax.rem(y, 2) * (3 - 2 * x)
    return ((z * 4 + y) * 4 + x) * 2 + 1 - core


def body(
    drv_in, stiff_in, coup_in, fric_in, edge_in, nbr_in, send_in,
    owner_in, pcell_in, obs_in, look_in,
    vel_out, adj_out, lf_out,
    drv, stiff, coup, fric, edge, nbr, send, owner, pcell, obs, look,
    vel, logf, inverse_diag, partial, home_send, home_logf, home_inverse, home_partial,
    last_out, last_in, home_selt,
    mhi, mlo, thi, tlo, sel, selt, frc, wts, sums, out, got, snd, rcv,
    ssem, rsem, asem, gsem, lsem, msem, isem, osem, hsem, psem, qsem, ysem, zsem,
):
    n = lax.axis_size("dom")
    me = lax.axis_index("dom")
    mine = part_at(me)
    away = place_of(me)
    cells = drv.shape[1]
    halo = send.shape[1]
    ext = cells + 4 * halo

    loads = [
        pltpu.make_async_copy(src, dst, lsem.at[k])
        for k, (src, dst) in enumerate(
            [
                (owner_in, owner), (pcell_in, pcell), (obs_in, obs), (look_in, look),
                (send_in, home_send),
            ]
        )
    ]
    for c in loads:
        c.start()
    moves = [
        pltpu.make_async_remote_copy(
            src, dst, msem.at[k], isem.at[k], device_id=(away,), device_id_type=MESH
        )
        for k, (src, dst) in enumerate(
            [
                (send_in, send), (nbr_in, nbr), (edge_in, edge), (stiff_in, stiff),
                (coup_in, coup), (fric_in, fric), (drv_in, drv),
            ]
        )
    ]
    partners = [
        [place_of(lax.rem(mine + sign * o + n, n)) for o in OFFSETS] for sign in (1, -1)
    ]

    barrier = pltpu.get_barrier_semaphore()

    line = lax.div(me, 8) * 8
    y_mates = [lax.div(me, 32) * 32 + lax.rem(me + 8 * k, 32) for k in (1, 2, 3)]
    z_mates = [lax.rem(me + 32 * k, n) for k in (1, 2, 3)]
    near = [line + lax.rem(me + k, 8) for k in range(1, 8)]
    near += y_mates + z_mates + partners[0] + [away, mine]
    for peer in near:
        pl.semaphore_signal(barrier, inc=1, device_id=(peer,), device_id_type=MESH)

    pl.semaphore_wait(barrier, len(near))
    for c in moves:
        c.start()
    for peer in y_mates:
        pl.semaphore_signal(ysem, inc=1, device_id=(peer,), device_id_type=MESH)

    for c in loads:
        c.wait()
    own_row = owner[...].astype(f32)
    eye = iota((128, 128), 0) == iota((128, 128), 1)
    own_col = jnp.sum(jnp.where(eye, own_row, 0.0), axis=1, keepdims=True)
    before = (own_col == own_row) & (iota((128, 128), 0) < iota((128, 128), 1))
    rank = jnp.sum(jnp.where(before, 1.0, 0.0), axis=0, keepdims=True)
    first_line = place_of(owner[...]) * 8 + rank.astype(jnp.int32)
    lines = jnp.concatenate([first_line + 2 * q for q in range(4)], axis=1)
    data = jnp.concatenate(
        [pcell[...].astype(f32), obs[...], look[0], look[1]], axis=0
    )
    hi, lo = split(data)
    data = jnp.concatenate([hi, lo], axis=1).astype(bf16)
    for b in range(8):
        hit = iota((128, 512), 0) + 128 * b == lines
        placed = mm(jnp.where(hit, 1.0, 0.0).astype(bf16), data)
        placed = placed[:, 0:128] + placed[:, 128:256]
        out[b * 16 : (b + 1) * 16] = placed.reshape(16, 8, 128)

    pl.semaphore_wait(ysem, 3)
    for peer in z_mates:
        pl.semaphore_signal(zsem, inc=1, device_id=(peer,), device_id_type=MESH)
    def row_copy(r):
        peer = lax.rem(me + r, n)
        return pltpu.make_async_remote_copy(
            out.at[peer], got.at[me], asem.at[0], gsem.at[0],
            device_id=(peer,), device_id_type=MESH,
        )

    def row_starts(b, carry):
        for k in range(9):
            row_copy(b * 9 + 1 + k).start()
        return carry

    got[me] = out[me]
    pl.semaphore_wait(zsem, 3)
    lax.fori_loop(0, (n - 2) // 9, row_starts, 0)
    row_copy(n - 1).start()

    moves[0].wait_recv()
    for j in range(4):
        hit = iota((cells, halo), 0) == send[j : j + 1, :]
        sel[:, j * halo : (j + 1) * halo] = jnp.where(hit, 1.0, 0.0).astype(bf16)
    for c in moves[1:]:
        c.wait_recv()

    weights = jnp.where(nbr[...] != iota((8, cells), 1), edge[...], 0.0)
    wts[...] = weights
    rowsum = jnp.sum(weights, axis=0, keepdims=True)
    layer = iota((8, cells), 0)
    links = jnp.where((layer == 0) | (layer == LAYERS - 1), 1.0, 2.0)
    coupling = coup[...]
    static_diag = stiff[...] + rowsum + coupling * links

    frc[...] = jnp.zeros_like(frc)
    frc[0:LAYERS, :] = drv[0:LAYERS, :]
    frc[8 : 8 + LAYERS, :] = drv[LAYERS : 2 * LAYERS, :]

    def inverse(lf):
        diag = static_diag + jnp.where(layer == LAYERS - 1, jnp.exp(lf), 0.0)
        return jnp.where(layer < LAYERS, 1.0 / diag, 0.0)

    def scaled(x, inv):
        return jnp.concatenate([x[0:8] * inv, x[8:16] * inv], axis=0)

    def vertical(x):
        return coupling * (pltpu.roll(x, 1, 0) + pltpu.roll(x, 15, 0))

    def build():
        name = nbr[...]
        total = weights
        again = jnp.zeros(name.shape, jnp.int32)
        for shift in range(1, 8):
            same = pltpu.roll(name, shift, 0) == name
            total = total + jnp.where(same, pltpu.roll(weights, shift, 0), 0.0)
            again = again + jnp.where(same & (layer >= shift), 1, 0)
        name = jnp.where(again > 0, -1, name).astype(jnp.int16)
        part_hi, part_lo = split(total)
        part_hi = part_hi.astype(bf16)
        part_lo = part_lo.astype(bf16)
        width = 256
        for c in range(0, cells, width):
            def line_of(a, e):
                return jnp.broadcast_to(a[e : e + 1, c : c + width], (16, width))

            names = [line_of(name, e) for e in range(8)]
            his = [line_of(part_hi, e) for e in range(8)]
            los = [line_of(part_lo, e) for e in range(8)]

            def rows_of(b, carry):
                base = pl.multiple_of(b * 16, 16)
                rows = (iota((16, width), 0) + base).astype(jnp.int16)
                hi = jnp.zeros((16, width), bf16)
                lo = jnp.zeros((16, width), bf16)
                for e in range(8):
                    hit = rows == names[e]
                    hi = jnp.where(hit, his[e], hi)
                    lo = jnp.where(hit, los[e], lo)
                mhi[pl.ds(base, 16), c : c + width] = hi
                mlo[pl.ds(base, 16), c : c + width] = lo
                return carry

            lax.fori_loop(0, ext // 16, rows_of, 0, unroll=8)

    def rows_done(sem, ref):
        all_but_one = ref.at[pl.ds(0, n - 1)]
        pltpu.make_async_copy(all_but_one, all_but_one, sem.at[0]).wait()

    def pixels(g, acc):
        lhs = []
        rhs = []
        for s in range(16):
            blk = got[g * 16 + s]
            for slot in range(2):
                idx = blk[slot : slot + 1].astype(jnp.int32)
                ob = blk[2 + slot : 3 + slot]
                lx = blk[4 + slot : 5 + slot]
                ly = blk[6 + slot : 7 + slot]
                low = jnp.broadcast_to((idx & 127).astype(jnp.int16), (128, 128))
                low = iota((128, 128), 0).astype(jnp.int16) == low
                rhs.append(jnp.where(low, jnp.ones_like(low, bf16), jnp.zeros_like(low, bf16)))
                high = iota((8, 128), 0) == (idx >> 7)
                vals = [
                    jnp.where(high, q, 0.0)
                    for q in (lx * lx, lx * ly, ly * ly, lx * ob, ly * ob)
                ]
                lhs.append(stacked(jnp.concatenate(vals, axis=0)))
        return acc + mm(jnp.concatenate(lhs, axis=1), jnp.concatenate(rhs, axis=1), NT)

    def copies(i, sign):
        return [
            pltpu.make_async_remote_copy(
                snd.at[i, j],
                rcv.at[i, j],
                ssem.at[i],
                rsem.at[i],
                device_id=(partners[0 if sign == 1 else 1][j],),
                device_id_type=MESH,
            )
            for j in range(4)
        ]

    def push(i, piece, sign):
        cps = copies(i, sign)
        for j in ORDER:
            snd[i, j] = piece[:, j * halo : (j + 1) * halo]
            cps[j].start()

    def fetched(i):
        pltpu.make_async_copy(rcv.at[i], rcv.at[i], rsem.at[i]).wait()
        return stacked(jnp.concatenate([rcv[i, j] for j in range(4)], axis=1))

    def two(xs, hi, lo, dims=NN):
        a = mm(xs, hi, dims)
        return a[0:16] + a[16:32] + mm(xs[0:16], lo, dims)

    def fwd_send(i, xs):
        piece = mm(xs, sel[...])
        push(i, piece[0:16] + piece[16:32], 1)

    def fwd_own(xs):
        return two(xs, mhi[0:cells, :], mlo[0:cells, :])

    def fwd_halo(i):
        return two(fetched(i), mhi[cells:ext, :], mlo[cells:ext, :])

    def fwd(i, x, inv, extra=None):
        xs = stacked(x)
        fwd_send(i, xs)
        if extra is not None:
            extra()
        own = fwd_own(xs) + frc[...] + vertical(x)
        return scaled(own + fwd_halo(i), inv)

    def adj(i, x, source, inv, extra=None):
        xs = stacked(x)
        push(i, two(xs, thi[...], tlo[...]), -1)
        if extra is not None:
            extra()
        own = two(xs, mhi[0:cells, :], mlo[0:cells, :], NT) + source + vertical(x)
        a = mm(fetched(i), selt[...])
        return scaled(own + a[0:16] + a[16:32], inv)

    lf = jnp.log(fric[...])
    inv = inverse(lf)
    x = scaled(frc[...], inv)

    def during_first():
        build()

    halves = []

    def during_second():
        thi[...] = mhi[cells:ext, :].astype(f32).T.astype(bf16)
        tlo[...] = mlo[cells:ext, :].astype(f32).T.astype(bf16)
        rows_done(gsem, got)
        halves.append(lax.fori_loop(0, n // 32, pixels, jnp.zeros((80, 128), f32)))

    def during_third():
        acc = lax.fori_loop(n // 32, n // 16, pixels, halves[0])
        tot = acc[0:40] + acc[40:80]
        for q in range(5):
            for h in range(8):
                line = q * 8 + h
                sums[q : q + 1, h * 128 : (h + 1) * 128] = tot[line : line + 1]

    x = fwd(0, x, inv, during_first)
    x = fwd(1, x, inv, during_second)
    x = fwd(2, x, inv, during_third)

    def source_of(x):
        mx = jnp.sum(x[0:8], axis=0, keepdims=True) / LAYERS
        my = jnp.sum(x[8:16], axis=0, keepdims=True) / LAYERS
        px = (sums[0:1, :] * mx + sums[1:2, :] * my - sums[3:4, :]) / LAYERS
        py = (sums[1:2, :] * mx + sums[2:3, :] * my - sums[4:5, :]) / LAYERS
        return jnp.concatenate(
            [jnp.broadcast_to(px, (8, cells)), jnp.broadcast_to(py, (8, cells))], axis=0
        )

    def stepped(lf, lam, x):
        grad = -(lam[4:5] * x[4:5] + lam[12:13] * x[12:13])
        return lf - RATE * jnp.tanh(jnp.exp(lf) * grad)

    homeward = [
        pltpu.make_async_remote_copy(
            src, dst, osem.at[k], hsem.at[k], device_id=(mine,), device_id_type=MESH
        )
        for k, (src, dst) in enumerate(
            [
                (vel, vel_out), (logf, home_logf), (inverse_diag, home_inverse),
                (partial, home_partial),
            ]
        )
    ]

    source = source_of(x)
    lam = scaled(source, inv)
    held = []

    def early_send():
        selt[...] = sel[...].astype(f32).T.astype(bf16)
        fwd_send(6, stacked(x))

    def early_across():
        held.append(fwd_own(stacked(x)) + fwd_halo(6) + frc[...] + vertical(x))

    lam = adj(3, lam, source, inv, early_send)
    lam = adj(4, lam, source, inv, early_across)
    lam = adj(5, lam, source, inv)
    lf = stepped(lf, lam, x)

    inv = inverse(lf)
    logf[...] = lf
    inverse_diag[...] = inv
    homeward[1].start()
    homeward[2].start()
    x = scaled(held[0], inv)
    x = lax.fori_loop(7, 10, lambda i, v: fwd(i, v, inv), x)
    source = source_of(x)
    lam = scaled(source, inv)
    vel[0:LAYERS, :] = x[0:LAYERS]
    vel[LAYERS : 2 * LAYERS, :] = x[8 : 8 + LAYERS]
    homeward[0].start()

    def home_selection():
        for j in range(4):
            hit = iota((cells, halo), 0) == home_send[j : j + 1, :]
            home_selt[j * halo : (j + 1) * halo, :] = jnp.where(hit, 1.0, 0.0).T.astype(bf16)

    lam = adj(10, lam, source, inv, home_selection)
    lam = adj(11, lam, source, inv)

    xs = stacked(lam)
    piece = two(xs, thi[...], tlo[...])
    homes = [lax.rem(mine - o + n, n) for o in OFFSETS]

    def last_copy(j):
        return pltpu.make_async_remote_copy(
            last_out.at[j], last_in.at[j], psem.at[j], qsem.at[j],
            device_id=(homes[j],), device_id_type=MESH,
        )

    for j in ORDER:
        last_out[j] = piece[:, j * halo : (j + 1) * halo]

        @pl.when(homes[j] != me)
        def _():
            last_copy(j).start()

        @pl.when(homes[j] == me)
        def _():
            pltpu.make_async_copy(last_out.at[j], last_in.at[j], qsem.at[j]).start()

    own = two(xs, mhi[0:cells, :], mlo[0:cells, :], NT) + source + vertical(lam)
    partial[...] = scaled(own, inv)
    homeward[3].start()

    homeward[0].wait_recv()
    homeward[1].wait_recv()
    homeward[2].wait_recv()
    for j in ORDER:
        pltpu.make_async_copy(last_in.at[j], last_in.at[j], qsem.at[j]).wait()
    ys = stacked(jnp.concatenate([last_in[j] for j in range(4)], axis=1))
    a = mm(ys, home_selt[...])
    add = scaled(a[0:16] + a[16:32], home_inverse[...])
    homeward[3].wait_recv()
    lam = home_partial[...] + add
    adj_out[0:LAYERS, :] = lam[0:LAYERS]
    adj_out[LAYERS : 2 * LAYERS, :] = lam[8 : 8 + LAYERS]
    top, low = vel_out[4:5, :], vel_out[9:10, :]
    grad = -(lam[4:5] * top + lam[12:13] * low)
    lf = home_logf[...]
    lf_out[...] = lf - RATE * jnp.tanh(jnp.exp(lf) * grad)

    def drain(i, carry):
        pltpu.make_async_copy(snd.at[i], snd.at[i], ssem.at[i]).wait()
        return carry

    lax.fori_loop(0, ROUNDS, drain, 0)
    rows_done(asem, out)
    for c in moves:
        c.wait_send()
    for c in homeward:
        c.wait_send()
    for j in range(4):

        @pl.when(homes[j] != me)
        def _():
            last_copy(j).wait_send()


def finish(vel_in, adj_in, lf_in, vel_out, adj_out, lf_out, sem):
    cps = [
        pltpu.make_async_copy(src, dst, sem.at[k])
        for k, (src, dst) in enumerate(
            [(vel_in, vel_out), (adj_in, adj_out), (lf_in, lf_out)]
        )
    ]
    for c in cps:
        c.start()
    for c in cps:
        c.wait()


def local(
    driving_force, stiffness, coupling, friction, edge_coef, neighbours,
    send_cells, row_owner, pixel_cell, observed, look_vector,
):
    n = lax.axis_size("dom")
    cells = driving_force.shape[1]
    halo = send_cells.shape[1]
    ext = cells + 4 * halo
    here = pl.BlockSpec(memory_space=pltpu.HBM)
    vmem = pl.BlockSpec(memory_space=pltpu.VMEM)
    rows, pixels = pixel_cell.shape
    results = (
        jax.ShapeDtypeStruct(driving_force.shape, f32),
        jax.ShapeDtypeStruct(driving_force.shape, f32),
        jax.ShapeDtypeStruct((1, cells), f32),
    )
    vel, adj, lf = pl.pallas_call(
        body,
        out_shape=results,
        in_specs=[here] * 11,
        out_specs=(vmem, vmem, vmem),
        scratch_shapes=[
            pltpu.VMEM(driving_force.shape, f32),
            pltpu.VMEM((1, cells), f32),
            pltpu.VMEM((1, cells), f32),
            pltpu.VMEM((1, cells), f32),
            pltpu.VMEM(edge_coef.shape, f32),
            pltpu.VMEM(neighbours.shape, jnp.int32),
            pltpu.VMEM(send_cells.shape, jnp.int32),
            pltpu.VMEM((1, rows), jnp.int32),
            pltpu.VMEM((rows, pixels), jnp.int32),
            pltpu.VMEM((rows, pixels), f32),
            pltpu.VMEM((2, rows, pixels), f32),
            pltpu.VMEM(driving_force.shape, f32),
            pltpu.VMEM((1, cells), f32),
            pltpu.VMEM((8, cells), f32),
            pltpu.VMEM((16, cells), f32),
            pltpu.VMEM(send_cells.shape, jnp.int32),
            pltpu.VMEM((1, cells), f32),
            pltpu.VMEM((8, cells), f32),
            pltpu.VMEM((16, cells), f32),
            pltpu.VMEM((4, 16, halo), f32),
            pltpu.VMEM((4, 16, halo), f32),
            pltpu.VMEM((4 * halo, cells), bf16),
            pltpu.VMEM((ext, cells), bf16),
            pltpu.VMEM((ext, cells), bf16),
            pltpu.VMEM((cells, 4 * halo), bf16),
            pltpu.VMEM((cells, 4 * halo), bf16),
            pltpu.VMEM((cells, 4 * halo), bf16),
            pltpu.VMEM((4 * halo, cells), bf16),
            pltpu.VMEM((16, cells), f32),
            pltpu.VMEM((8, cells), f32),
            pltpu.VMEM((8, cells), f32),
            pltpu.VMEM((n, 8, 128), f32),
            pltpu.VMEM((n, 8, 128), f32),
            pltpu.VMEM((ROUNDS, 4, 16, halo), f32),
            pltpu.VMEM((ROUNDS, 4, 16, halo), f32),
            pltpu.SemaphoreType.DMA((ROUNDS,)),
            pltpu.SemaphoreType.DMA((ROUNDS,)),
            pltpu.SemaphoreType.DMA((1,)),
            pltpu.SemaphoreType.DMA((1,)),
            pltpu.SemaphoreType.DMA((5,)),
            pltpu.SemaphoreType.DMA((7,)),
            pltpu.SemaphoreType.DMA((7,)),
            pltpu.SemaphoreType.DMA((4,)),
            pltpu.SemaphoreType.DMA((4,)),
            pltpu.SemaphoreType.DMA((4,)),
            pltpu.SemaphoreType.DMA((4,)),
            pltpu.SemaphoreType.REGULAR,
            pltpu.SemaphoreType.REGULAR,
        ],
        compiler_params=pltpu.CompilerParams(
            collective_id=0, has_side_effects=True, vmem_limit_bytes=48 * 1024 * 1024
        ),
    )(*[
        pltpu.with_memory_space_constraint(a, pltpu.HBM)
        for a in (
            driving_force, stiffness[None, :], coupling[None, :], friction[None, :],
            edge_coef, neighbours, send_cells, row_owner.reshape(1, rows), pixel_cell,
            observed, look_vector,
        )
    ])
    vel, adj, lf = pl.pallas_call(
        finish,
        out_shape=results,
        in_specs=[vmem] * 3,
        out_specs=(here, here, here),
        scratch_shapes=[pltpu.SemaphoreType.DMA((3,))],
        compiler_params=pltpu.CompilerParams(vmem_limit_bytes=2 * 1024 * 1024),
    )(vel, adj, lf)
    return vel, adj, lf[0]


def solution(mesh):
    in_specs = (
        P(None, "dom"), P("dom"), P("dom"), P("dom"), P(None, "dom"), P(None, "dom"),
        P("dom", None), P("dom", None), P("dom", None), P("dom", None), P(None, "dom", None),
    )
    out_specs = (P(None, "dom"), P(None, "dom"), P("dom"))
    return jax.shard_map(local, mesh=mesh, in_specs=in_specs, out_specs=out_specs, check_vma=False)
```

```python
import jax
import jax.numpy as jnp
from jax import lax
from jax.experimental import pallas as pl
from jax.experimental.pallas import tpu as pltpu
from jax.sharding import PartitionSpec as P

SWEEPS = 4
STEPS = 2
OFFSETS = (1, -1, 2, -2)
ORDER = (2, 3, 0, 1)
RATE = 0.5
LAYERS = 5
ROUNDS = 12
MESH = pl.DeviceIdType.MESH
NT = (((1,), (1,)), ((), ()))
NN = (((1,), (0,)), ((), ()))
f32 = jnp.float32
bf16 = jnp.bfloat16


def split(x):
    hi = x.astype(bf16).astype(f32)
    return hi, x - hi


def stacked(x):
    hi, lo = split(x)
    return jnp.concatenate([hi, lo], axis=0).astype(bf16)


def mm(a, b, dims=NN):
    return lax.dot_general(a, b, dims, preferred_element_type=f32)


def iota(shape, dim):
    return lax.broadcasted_iota(jnp.int32, shape, dim)


def place_of(part):
    core = lax.rem(part, 2)
    chip = lax.div(part, 2)
    x = lax.rem(chip, 4)
    y = lax.rem(lax.div(chip, 4), 4)
    z = lax.div(chip, 16)
    x = x + lax.rem(y, 2) * (3 - 2 * x)
    y = y + lax.rem(z, 2) * (3 - 2 * y)
    return ((z * 4 + y) * 4 + x) * 2 + 1 - core


def part_at(device):
    core = lax.rem(device, 2)
    chip = lax.div(device, 2)
    x = lax.rem(chip, 4)
    y = lax.rem(lax.div(chip, 4), 4)
    z = lax.div(chip, 16)
    y = y + lax.rem(z, 2) * (3 - 2 * y)
    x = x + lax.rem(y, 2) * (3 - 2 * x)
    return ((z * 4 + y) * 4 + x) * 2 + 1 - core


def body(
    drv_in, stiff_in, coup_in, fric_in, edge_in, nbr_in, send_in,
    owner_in, pcell_in, obs_in, look_in,
    vel_out, adj_out, lf_out,
    drv, stiff, coup, fric, edge, nbr, send, owner, pcell, obs, look,
    vel, logf, inverse_diag, partial, home_send, home_logf, home_inverse, home_partial,
    last_out, last_in, home_selt,
    mhi, mlo, thi, tlo, sel, selt, frc, wts, sums, out, got, snd, rcv, snd8, rcv8,
    ssem, rsem, asem, gsem, lsem, msem, isem, osem, hsem, psem, qsem, ysem, zsem,
):
    n = lax.axis_size("dom")
    me = lax.axis_index("dom")
    mine = part_at(me)
    away = place_of(me)
    cells = drv.shape[1]
    halo = send.shape[1]
    ext = cells + 4 * halo

    loads = [
        pltpu.make_async_copy(src, dst, lsem.at[k])
        for k, (src, dst) in enumerate(
            [
                (owner_in, owner), (pcell_in, pcell), (obs_in, obs), (look_in, look),
                (send_in, home_send),
            ]
        )
    ]
    for c in loads:
        c.start()
    moves = [
        pltpu.make_async_remote_copy(
            src, dst, msem.at[k], isem.at[k], device_id=(away,), device_id_type=MESH
        )
        for k, (src, dst) in enumerate(
            [
                (send_in, send), (nbr_in, nbr), (edge_in, edge), (stiff_in, stiff),
                (coup_in, coup), (fric_in, fric), (drv_in, drv),
            ]
        )
    ]
    partners = [
        [place_of(lax.rem(mine + sign * o + n, n)) for o in OFFSETS] for sign in (1, -1)
    ]

    barrier = pltpu.get_barrier_semaphore()

    line = lax.div(me, 8) * 8
    y_mates = [lax.div(me, 32) * 32 + lax.rem(me + 8 * k, 32) for k in (1, 2, 3)]
    z_mates = [lax.rem(me + 32 * k, n) for k in (1, 2, 3)]
    near = [line + lax.rem(me + k, 8) for k in range(1, 8)]
    near += y_mates + z_mates + partners[0] + [away, mine]
    for peer in near:
        pl.semaphore_signal(barrier, inc=1, device_id=(peer,), device_id_type=MESH)

    pl.semaphore_wait(barrier, len(near))
    for c in moves:
        c.start()
    for peer in y_mates:
        pl.semaphore_signal(ysem, inc=1, device_id=(peer,), device_id_type=MESH)

    for c in loads:
        c.wait()
    own_row = owner[...].astype(f32)
    eye = iota((128, 128), 0) == iota((128, 128), 1)
    own_col = jnp.sum(jnp.where(eye, own_row, 0.0), axis=1, keepdims=True)
    before = (own_col == own_row) & (iota((128, 128), 0) < iota((128, 128), 1))
    rank = jnp.sum(jnp.where(before, 1.0, 0.0), axis=0, keepdims=True)
    first_line = place_of(owner[...]) * 8 + rank.astype(jnp.int32)
    lines = jnp.concatenate([first_line + 2 * q for q in range(4)], axis=1)
    data = jnp.concatenate(
        [pcell[...].astype(f32), obs[...], look[0], look[1]], axis=0
    )
    hi, lo = split(data)
    data = jnp.concatenate([hi, lo], axis=1).astype(bf16)
    for b in range(8):
        hit = iota((128, 512), 0) + 128 * b == lines
        placed = mm(jnp.where(hit, 1.0, 0.0).astype(bf16), data)
        placed = placed[:, 0:128] + placed[:, 128:256]
        out[b * 16 : (b + 1) * 16] = placed.reshape(16, 8, 128)

    pl.semaphore_wait(ysem, 3)
    for peer in z_mates:
        pl.semaphore_signal(zsem, inc=1, device_id=(peer,), device_id_type=MESH)
    def row_copy(r):
        peer = lax.rem(me + r, n)
        return pltpu.make_async_remote_copy(
            out.at[peer], got.at[me], asem.at[0], gsem.at[0],
            device_id=(peer,), device_id_type=MESH,
        )

    def row_starts(b, carry):
        for k in range(9):
            row_copy(b * 9 + 1 + k).start()
        return carry

    got[me] = out[me]
    pl.semaphore_wait(zsem, 3)
    lax.fori_loop(0, (n - 2) // 9, row_starts, 0)
    row_copy(n - 1).start()

    moves[0].wait_recv()
    for j in range(4):
        hit = iota((cells, halo), 0) == send[j : j + 1, :]
        sel[:, j * halo : (j + 1) * halo] = jnp.where(hit, 1.0, 0.0).astype(bf16)
    for c in moves[1:]:
        c.wait_recv()

    weights = jnp.where(nbr[...] != iota((8, cells), 1), edge[...], 0.0)
    wts[...] = weights
    rowsum = jnp.sum(weights, axis=0, keepdims=True)
    layer = iota((8, cells), 0)
    links = jnp.where((layer == 0) | (layer == LAYERS - 1), 1.0, 2.0)
    coupling = coup[...]
    static_diag = stiff[...] + rowsum + coupling * links

    frc[...] = jnp.zeros_like(frc)
    frc[0:LAYERS, :] = drv[0:LAYERS, :]
    frc[8 : 8 + LAYERS, :] = drv[LAYERS : 2 * LAYERS, :]

    def inverse(lf):
        diag = static_diag + jnp.where(layer == LAYERS - 1, jnp.exp(lf), 0.0)
        return jnp.where(layer < LAYERS, 1.0 / diag, 0.0)

    def scaled(x, inv):
        return jnp.concatenate([x[0:8] * inv, x[8:16] * inv], axis=0)

    def vertical(x):
        return coupling * (pltpu.roll(x, 1, 0) + pltpu.roll(x, 15, 0))

    def build():
        name = nbr[...]
        total = weights
        again = jnp.zeros(name.shape, jnp.int32)
        for shift in range(1, 8):
            same = pltpu.roll(name, shift, 0) == name
            total = total + jnp.where(same, pltpu.roll(weights, shift, 0), 0.0)
            again = again + jnp.where(same & (layer >= shift), 1, 0)
        name = jnp.where(again > 0, -1, name).astype(jnp.int16)
        part_hi, part_lo = split(total)
        part_hi = part_hi.astype(bf16)
        part_lo = part_lo.astype(bf16)
        width = 256
        for c in range(0, cells, width):
            def line_of(a, e):
                return jnp.broadcast_to(a[e : e + 1, c : c + width], (16, width))

            names = [line_of(name, e) for e in range(8)]
            his = [line_of(part_hi, e) for e in range(8)]
            los = [line_of(part_lo, e) for e in range(8)]

            def rows_of(b, carry):
                base = pl.multiple_of(b * 16, 16)
                rows = (iota((16, width), 0) + base).astype(jnp.int16)
                hi = jnp.zeros((16, width), bf16)
                lo = jnp.zeros((16, width), bf16)
                for e in range(8):
                    hit = rows == names[e]
                    hi = jnp.where(hit, his[e], hi)
                    lo = jnp.where(hit, los[e], lo)
                mhi[pl.ds(base, 16), c : c + width] = hi
                mlo[pl.ds(base, 16), c : c + width] = lo
                return carry

            lax.fori_loop(0, ext // 16, rows_of, 0, unroll=8)

    def rows_done(sem, ref):
        all_but_one = ref.at[pl.ds(0, n - 1)]
        pltpu.make_async_copy(all_but_one, all_but_one, sem.at[0]).wait()

    def pixels(g, acc):
        lhs = []
        rhs = []
        for s in range(16):
            blk = got[g * 16 + s]
            for slot in range(2):
                idx = blk[slot : slot + 1].astype(jnp.int32)
                ob = blk[2 + slot : 3 + slot]
                lx = blk[4 + slot : 5 + slot]
                ly = blk[6 + slot : 7 + slot]
                low = jnp.broadcast_to((idx & 127).astype(jnp.int16), (128, 128))
                low = iota((128, 128), 0).astype(jnp.int16) == low
                rhs.append(jnp.where(low, jnp.ones_like(low, bf16), jnp.zeros_like(low, bf16)))
                high = iota((8, 128), 0) == (idx >> 7)
                vals = [
                    jnp.where(high, q, 0.0)
                    for q in (lx * lx, lx * ly, ly * ly, lx * ob, ly * ob)
                ]
                lhs.append(stacked(jnp.concatenate(vals, axis=0)))
        return acc + mm(jnp.concatenate(lhs, axis=1), jnp.concatenate(rhs, axis=1), NT)

    def copies(i, sign):
        return [
            pltpu.make_async_remote_copy(
                snd.at[i, j],
                rcv.at[i, j],
                ssem.at[i],
                rsem.at[i],
                device_id=(partners[0 if sign == 1 else 1][j],),
                device_id_type=MESH,
            )
            for j in range(4)
        ]

    def push(i, piece, sign):
        cps = copies(i, sign)
        for j in ORDER:
            snd[i, j] = piece[:, j * halo : (j + 1) * halo]
            cps[j].start()

    def fetched(i):
        pltpu.make_async_copy(rcv.at[i], rcv.at[i], rsem.at[i]).wait()
        return stacked(jnp.concatenate([rcv[i, j] for j in range(4)], axis=1))

    def two(xs, hi, lo, dims=NN):
        a = mm(xs, hi, dims)
        return a[0:16] + a[16:32] + mm(xs[0:16], lo, dims)

    def fwd_send(i, xs):
        piece = mm(xs, sel[...])
        push(i, piece[0:16] + piece[16:32], 1)

    def fwd_own(xs):
        return two(xs, mhi[0:cells, :], mlo[0:cells, :])

    def fwd_halo(i):
        return two(fetched(i), mhi[cells:ext, :], mlo[cells:ext, :])

    def fwd(i, x, inv, extra=None):
        xs = stacked(x)
        fwd_send(i, xs)
        if extra is not None:
            extra()
        own = fwd_own(xs) + frc[...] + vertical(x)
        return scaled(own + fwd_halo(i), inv)

    def adj(i, x, source, inv, extra=None):
        xs = stacked(x)
        push(i, two(xs, thi[...], tlo[...]), -1)
        if extra is not None:
            extra()
        own = two(xs, mhi[0:cells, :], mlo[0:cells, :], NT) + source + vertical(x)
        a = mm(fetched(i), selt[...])
        return scaled(own + a[0:16] + a[16:32], inv)

    def adj_base(i, x, source, inv, extra=None):
        xs = stacked(x)
        piece = two(xs, thi[...], tlo[...])
        first = iota((8, 4 * halo), 0) < 4
        piece = jnp.where(first, pltpu.roll(piece[0:8], 7, 0), pltpu.roll(piece[8:16], 3, 0))
        for j in ORDER:
            snd8[i - 3, j] = piece[:, j * halo : (j + 1) * halo]
            pltpu.make_async_remote_copy(
                snd8.at[i - 3, j], rcv8.at[i - 3, j], ssem.at[i], rsem.at[i],
                device_id=(partners[1][j],), device_id_type=MESH,
            ).start()
        if extra is not None:
            extra()
        own = two(xs, mhi[0:cells, :], mlo[0:cells, :], NT) + source + vertical(x)
        pltpu.make_async_copy(rcv8.at[i - 3], rcv8.at[i - 3], rsem.at[i]).wait()
        ys = stacked(jnp.concatenate([rcv8[i - 3, j] for j in range(4)], axis=1))
        a = mm(ys, selt[...])
        a = a[0:8] + a[8:16]
        a = jnp.concatenate([pltpu.roll(a, 1, 0), pltpu.roll(a, 5, 0)], axis=0)
        return scaled(own + a, inv)

    lf = jnp.log(fric[...])
    inv = inverse(lf)
    x = scaled(frc[...], inv)

    def during_first():
        build()

    halves = []

    def during_second():
        thi[...] = mhi[cells:ext, :].astype(f32).T.astype(bf16)
        tlo[...] = mlo[cells:ext, :].astype(f32).T.astype(bf16)
        rows_done(gsem, got)
        halves.append(lax.fori_loop(0, n // 32, pixels, jnp.zeros((80, 128), f32)))

    def during_third():
        acc = lax.fori_loop(n // 32, n // 16, pixels, halves[0])
        tot = acc[0:40] + acc[40:80]
        for q in range(5):
            for h in range(8):
                line = q * 8 + h
                sums[q : q + 1, h * 128 : (h + 1) * 128] = tot[line : line + 1]

    x = fwd(0, x, inv, during_first)
    x = fwd(1, x, inv, during_second)
    x = fwd(2, x, inv, during_third)

    def source_of(x):
        mx = jnp.sum(x[0:8], axis=0, keepdims=True) / LAYERS
        my = jnp.sum(x[8:16], axis=0, keepdims=True) / LAYERS
        px = (sums[0:1, :] * mx + sums[1:2, :] * my - sums[3:4, :]) / LAYERS
        py = (sums[1:2, :] * mx + sums[2:3, :] * my - sums[4:5, :]) / LAYERS
        return jnp.concatenate(
            [jnp.broadcast_to(px, (8, cells)), jnp.broadcast_to(py, (8, cells))], axis=0
        )

    def stepped(lf, lam, x):
        grad = -(lam[4:5] * x[4:5] + lam[12:13] * x[12:13])
        return lf - RATE * jnp.tanh(jnp.exp(lf) * grad)

    homeward = [
        pltpu.make_async_remote_copy(
            src, dst, osem.at[k], hsem.at[k], device_id=(mine,), device_id_type=MESH
        )
        for k, (src, dst) in enumerate(
            [
                (vel, vel_out), (logf, home_logf), (inverse_diag, home_inverse),
                (partial, home_partial),
            ]
        )
    ]

    source = source_of(x)
    lam = scaled(source, inv)
    held = []

    def early_send():
        selt[...] = sel[...].astype(f32).T.astype(bf16)
        fwd_send(6, stacked(x))

    def early_across():
        held.append(fwd_own(stacked(x)) + fwd_halo(6) + frc[...] + vertical(x))

    lam = adj_base(3, lam, source, inv, early_send)
    lam = adj_base(4, lam, source, inv, early_across)
    lam = adj_base(5, lam, source, inv)
    lf = stepped(lf, lam, x)

    inv = inverse(lf)
    logf[...] = lf
    inverse_diag[...] = inv
    homeward[1].start()
    homeward[2].start()
    x = scaled(held[0], inv)
    x = lax.fori_loop(7, 10, lambda i, v: fwd(i, v, inv), x)
    source = source_of(x)
    lam = scaled(source, inv)
    vel[0:LAYERS, :] = x[0:LAYERS]
    vel[LAYERS : 2 * LAYERS, :] = x[8 : 8 + LAYERS]
    homeward[0].start()

    def home_selection():
        for j in range(4):
            hit = iota((cells, halo), 0) == home_send[j : j + 1, :]
            home_selt[j * halo : (j + 1) * halo, :] = jnp.where(hit, 1.0, 0.0).T.astype(bf16)

    lam = adj(10, lam, source, inv, home_selection)
    lam = adj(11, lam, source, inv)

    xs = stacked(lam)
    piece = two(xs, thi[...], tlo[...])
    homes = [lax.rem(mine - o + n, n) for o in OFFSETS]

    def last_copy(j):
        return pltpu.make_async_remote_copy(
            last_out.at[j], last_in.at[j], psem.at[j], qsem.at[j],
            device_id=(homes[j],), device_id_type=MESH,
        )

    for j in ORDER:
        last_out[j] = piece[:, j * halo : (j + 1) * halo]

        @pl.when(homes[j] != me)
        def _():
            last_copy(j).start()

        @pl.when(homes[j] == me)
        def _():
            pltpu.make_async_copy(last_out.at[j], last_in.at[j], qsem.at[j]).start()

    own = two(xs, mhi[0:cells, :], mlo[0:cells, :], NT) + source + vertical(lam)
    partial[...] = scaled(own, inv)
    homeward[3].start()

    homeward[0].wait_recv()
    homeward[1].wait_recv()
    homeward[2].wait_recv()
    for j in ORDER:
        pltpu.make_async_copy(last_in.at[j], last_in.at[j], qsem.at[j]).wait()
    ys = stacked(jnp.concatenate([last_in[j] for j in range(4)], axis=1))
    a = mm(ys, home_selt[...])
    add = scaled(a[0:16] + a[16:32], home_inverse[...])
    homeward[3].wait_recv()
    lam = home_partial[...] + add
    adj_out[0:LAYERS, :] = lam[0:LAYERS]
    adj_out[LAYERS : 2 * LAYERS, :] = lam[8 : 8 + LAYERS]
    top, low = vel_out[4:5, :], vel_out[9:10, :]
    grad = -(lam[4:5] * top + lam[12:13] * low)
    lf = home_logf[...]
    lf_out[...] = lf - RATE * jnp.tanh(jnp.exp(lf) * grad)

    def drain(i, carry):
        pltpu.make_async_copy(snd.at[i], snd.at[i], ssem.at[i]).wait()
        return carry

    lax.fori_loop(0, 3, drain, 0)
    for i in range(3, 6):
        pltpu.make_async_copy(snd8.at[i - 3], snd8.at[i - 3], ssem.at[i]).wait()
    lax.fori_loop(6, ROUNDS, drain, 0)
    rows_done(asem, out)
    for c in moves:
        c.wait_send()
    for c in homeward:
        c.wait_send()
    for j in range(4):

        @pl.when(homes[j] != me)
        def _():
            last_copy(j).wait_send()


def finish(vel_in, adj_in, lf_in, vel_out, adj_out, lf_out, sem):
    cps = [
        pltpu.make_async_copy(src, dst, sem.at[k])
        for k, (src, dst) in enumerate(
            [(vel_in, vel_out), (adj_in, adj_out), (lf_in, lf_out)]
        )
    ]
    for c in cps:
        c.start()
    for c in cps:
        c.wait()


def local(
    driving_force, stiffness, coupling, friction, edge_coef, neighbours,
    send_cells, row_owner, pixel_cell, observed, look_vector,
):
    n = lax.axis_size("dom")
    cells = driving_force.shape[1]
    halo = send_cells.shape[1]
    ext = cells + 4 * halo
    here = pl.BlockSpec(memory_space=pltpu.HBM)
    vmem = pl.BlockSpec(memory_space=pltpu.VMEM)
    rows, pixels = pixel_cell.shape
    results = (
        jax.ShapeDtypeStruct(driving_force.shape, f32),
        jax.ShapeDtypeStruct(driving_force.shape, f32),
        jax.ShapeDtypeStruct((1, cells), f32),
    )
    vel, adj, lf = pl.pallas_call(
        body,
        out_shape=results,
        in_specs=[here] * 11,
        out_specs=(vmem, vmem, vmem),
        scratch_shapes=[
            pltpu.VMEM(driving_force.shape, f32),
            pltpu.VMEM((1, cells), f32),
            pltpu.VMEM((1, cells), f32),
            pltpu.VMEM((1, cells), f32),
            pltpu.VMEM(edge_coef.shape, f32),
            pltpu.VMEM(neighbours.shape, jnp.int32),
            pltpu.VMEM(send_cells.shape, jnp.int32),
            pltpu.VMEM((1, rows), jnp.int32),
            pltpu.VMEM((rows, pixels), jnp.int32),
            pltpu.VMEM((rows, pixels), f32),
            pltpu.VMEM((2, rows, pixels), f32),
            pltpu.VMEM(driving_force.shape, f32),
            pltpu.VMEM((1, cells), f32),
            pltpu.VMEM((8, cells), f32),
            pltpu.VMEM((16, cells), f32),
            pltpu.VMEM(send_cells.shape, jnp.int32),
            pltpu.VMEM((1, cells), f32),
            pltpu.VMEM((8, cells), f32),
            pltpu.VMEM((16, cells), f32),
            pltpu.VMEM((4, 16, halo), f32),
            pltpu.VMEM((4, 16, halo), f32),
            pltpu.VMEM((4 * halo, cells), bf16),
            pltpu.VMEM((ext, cells), bf16),
            pltpu.VMEM((ext, cells), bf16),
            pltpu.VMEM((cells, 4 * halo), bf16),
            pltpu.VMEM((cells, 4 * halo), bf16),
            pltpu.VMEM((cells, 4 * halo), bf16),
            pltpu.VMEM((4 * halo, cells), bf16),
            pltpu.VMEM((16, cells), f32),
            pltpu.VMEM((8, cells), f32),
            pltpu.VMEM((8, cells), f32),
            pltpu.VMEM((n, 8, 128), f32),
            pltpu.VMEM((n, 8, 128), f32),
            pltpu.VMEM((ROUNDS, 4, 16, halo), f32),
            pltpu.VMEM((ROUNDS, 4, 16, halo), f32),
            pltpu.VMEM((3, 4, 8, halo), f32),
            pltpu.VMEM((3, 4, 8, halo), f32),
            pltpu.SemaphoreType.DMA((ROUNDS,)),
            pltpu.SemaphoreType.DMA((ROUNDS,)),
            pltpu.SemaphoreType.DMA((1,)),
            pltpu.SemaphoreType.DMA((1,)),
            pltpu.SemaphoreType.DMA((5,)),
            pltpu.SemaphoreType.DMA((7,)),
            pltpu.SemaphoreType.DMA((7,)),
            pltpu.SemaphoreType.DMA((4,)),
            pltpu.SemaphoreType.DMA((4,)),
            pltpu.SemaphoreType.DMA((4,)),
            pltpu.SemaphoreType.DMA((4,)),
            pltpu.SemaphoreType.REGULAR,
            pltpu.SemaphoreType.REGULAR,
        ],
        compiler_params=pltpu.CompilerParams(
            collective_id=0, has_side_effects=True, vmem_limit_bytes=48 * 1024 * 1024
        ),
    )(*[
        pltpu.with_memory_space_constraint(a, pltpu.HBM)
        for a in (
            driving_force, stiffness[None, :], coupling[None, :], friction[None, :],
            edge_coef, neighbours, send_cells, row_owner.reshape(1, rows), pixel_cell,
            observed, look_vector,
        )
    ])
    vel, adj, lf = pl.pallas_call(
        finish,
        out_shape=results,
        in_specs=[vmem] * 3,
        out_specs=(here, here, here),
        scratch_shapes=[pltpu.SemaphoreType.DMA((3,))],
        compiler_params=pltpu.CompilerParams(vmem_limit_bytes=2 * 1024 * 1024),
    )(vel, adj, lf)
    return vel, adj, lf[0]


def solution(mesh):
    in_specs = (
        P(None, "dom"), P("dom"), P("dom"), P("dom"), P(None, "dom"), P(None, "dom"),
        P("dom", None), P("dom", None), P("dom", None), P("dom", None), P(None, "dom", None),
    )
    out_specs = (P(None, "dom"), P(None, "dom"), P("dom"))
    return jax.shard_map(local, mesh=mesh, in_specs=in_specs, out_specs=out_specs, check_vma=False)
```
